32 devices in a mesh: fsdp: 4 (over y, x), seq: 8 (over z, core).
Axes of the slice: x: 2, y: 2, z: 4, core: 2. Of those that a mesh axis runs over, the one named last changes fastest.
Arguments:
- tokens: bfloat16 [2, 4, 2048, 2048], P(None, 'fsdp', 'seq'), may hold values from -6 to 6
- positions: int32 [2, 4, 2048], P(None, 'fsdp', 'seq'), may hold values from 0 to 2045, as said below
- out_grad: bfloat16 [2, 4, 2048, 2048], P(None, 'fsdp', 'seq'), may hold values from -6 to 6
- w_query: bfloat16 [2048, 2048], P(('fsdp', 'seq')), may hold values from -0.125 to 0.125
- w_key: bfloat16 [2048, 2048], P(('fsdp', 'seq')), may hold values from -0.125 to 0.125
- w_value: bfloat16 [2048, 2048], P(('fsdp', 'seq')), may hold values from -0.125 to 0.125
- w_output: bfloat16 [2048, 2048], P(('fsdp', 'seq')), may hold values from -0.125 to 0.125
- query_gain: bfloat16 [2048], P(('fsdp', 'seq')), may hold values from 0.5 to 1.5
- key_gain: bfloat16 [2048], P(('fsdp', 'seq')), may hold values from 0.5 to 1.5
- attn_gain: bfloat16 [2048], P(('fsdp', 'seq')), may hold values from 0.5 to 1.5
- w_gate: bfloat16 [2048, 8192], P(('fsdp', 'seq')), may hold values from -0.125 to 0.125
- w_up: bfloat16 [2048, 8192], P(('fsdp', 'seq')), may hold values from -0.125 to 0.125
- w_down: bfloat16 [8192, 2048], P(('fsdp', 'seq')), may hold values from -0.0625 to 0.0625
- mlp_gain: bfloat16 [2048], P(('fsdp', 'seq')), may hold values from 0.5 to 1.5
Outputs:
- mixed: bfloat16 [2, 4, 2048, 2048], P(None, 'fsdp', 'seq')
- input_grad: bfloat16 [2, 4, 2048, 2048], P(None, 'fsdp', 'seq')
- grad_w_query: float32 [2048, 2048], P(('fsdp', 'seq'))
- grad_w_key: float32 [2048, 2048], P(('fsdp', 'seq'))
- grad_w_value: float32 [2048, 2048], P(('fsdp', 'seq'))
- grad_w_output: float32 [2048, 2048], P(('fsdp', 'seq'))
- grad_query_gain: float32 [2048], P(('fsdp', 'seq'))
- grad_key_gain: float32 [2048], P(('fsdp', 'seq'))
- grad_attn_gain: float32 [2048], P(('fsdp', 'seq'))
- grad_w_gate: float32 [2048, 8192], P(('fsdp', 'seq'))
- grad_w_up: float32 [2048, 8192], P(('fsdp', 'seq'))
- grad_w_down: float32 [8192, 2048], P(('fsdp', 'seq'))
- grad_mlp_gain: float32 [2048], P(('fsdp', 'seq'))
The draws below stay inside these ranges and needn't reach their ends.
Inputs may be any that keep to these rules, and one draw needn't show every extreme that they name: `positions`: positions count from 0 at the first token of each document; a sequence holds three documents back to back, the middle one beginning among its first 256 tokens and ending among its last 256. Some sequence reaches the largest position.
All inputs are finite; a program needn't handle non-finite values.
Results may differ from the reference program's by a relative error of at most 0.025.
Values may be sent and summed in bfloat16 or wider, within the bound.
No kernel may reach another device: no remote copies, remote signals or barrier semaphores. Data moves between devices by JAX's collectives and lax.ppermute only.
A program may use at most 512 MiB of HBM per device.

```python
import jax
import jax.numpy as jnp
from jax import lax

D = 2048
HEADS = 16
HEAD_DIM = 128
FF = 8192
SEQ_LEN = 2048
MICRO = 2
SEQS = 4
TOK_SEQ = 256


def draw_positions(key, part):
    count_all = MICRO * SEQS
    first_key = jax.random.fold_in(key, 11)
    second_key = jax.random.fold_in(key, 23)
    first_cut = jax.random.randint(first_key, (count_all, 1), 1, TOK_SEQ)
    second_cut = jax.random.randint(second_key, (count_all, 1), SEQ_LEN - TOK_SEQ + 1, SEQ_LEN)
    row_ids = jnp.arange(count_all, dtype=jnp.int32)[:, None]
    first_cut = jnp.where(row_ids == 0, 1, first_cut)
    second_cut = jnp.where(row_ids == 0, SEQ_LEN - 1, second_cut)
    places = jnp.arange(SEQ_LEN, dtype=jnp.int32)[None, :]
    begins = jnp.where(places < first_cut, 0, jnp.where(places < second_cut, first_cut, second_cut))
    return (places - begins).astype(jnp.int32).reshape(MICRO, SEQS, SEQ_LEN)


def level_of(own_key, shape, split, least, largest):
    factor_of, own = 1.0, jax.random.fold_in(own_key, 6)
    for position, shards_of in split:
        draws = jnp.exp(jax.random.uniform(jax.random.fold_in(own, position), (shards_of,), jnp.float32, least / len(split), largest / len(split)))
        factor_of = factor_of * jnp.repeat(draws, shape[position] // shards_of).reshape([-1 if axis == position else 1 for axis in range(len(shape))])
    return factor_of


def bell_draw(stream_key, dims, deviation, reach, split=(), kind=jnp.bfloat16):
    entries = deviation * jax.random.normal(stream_key, dims, jnp.float32)
    if split:
        entries = entries * level_of(stream_key, dims, split, -0.22, 0.18)
    return jnp.clip(entries, -reach, reach).astype(kind)


def setup_inputs(seed: int = 0) -> dict:
    key_of = jax.random.split(jax.random.key(seed), 15)
    return {
        "tokens": bell_draw(key_of[0], (MICRO, SEQS, SEQ_LEN, D), 1.0, 6.0, ((1, 4), (2, 8))),
        "positions": draw_positions(jax.random.fold_in(key_of[14], 71), 0),
        "out_grad": bell_draw(key_of[2], (MICRO, SEQS, SEQ_LEN, D), 1.0, 6.0, ((1, 4), (2, 8))),
        "w_query": bell_draw(key_of[3], (D, D), D ** -0.5, 0.125, ((0, 32),)),
        "w_key": bell_draw(key_of[4], (D, D), D ** -0.5, 0.125, ((0, 32),)),
        "w_value": bell_draw(key_of[5], (D, D), D ** -0.5, 0.125, ((0, 32),)),
        "w_output": bell_draw(key_of[6], (D, D), D ** -0.5, 0.125, ((0, 32),)),
        "query_gain": jnp.clip(1.0 + 0.1 * jax.random.normal(key_of[7], (D,), jnp.float32), 0.5, 1.5).astype(jnp.bfloat16),
        "key_gain": jnp.clip(1.0 + 0.1 * jax.random.normal(key_of[8], (D,), jnp.float32), 0.5, 1.5).astype(jnp.bfloat16),
        "attn_gain": jnp.clip(1.0 + 0.1 * jax.random.normal(key_of[9], (D,), jnp.float32), 0.5, 1.5).astype(jnp.bfloat16),
        "w_gate": bell_draw(key_of[10], (D, FF), D ** -0.5, 0.125, ((0, 32),)),
        "w_up": bell_draw(key_of[11], (D, FF), D ** -0.5, 0.125, ((0, 32),)),
        "w_down": bell_draw(key_of[12], (FF, D), FF ** -0.5, 0.0625, ((0, 32),)),
        "mlp_gain": jnp.clip(1.0 + 0.1 * jax.random.normal(key_of[13], (D,), jnp.float32), 0.5, 1.5).astype(jnp.bfloat16),
    }


@jax.custom_vjp
def low(v):
    return lax.optimization_barrier(v.astype(jnp.bfloat16)).astype(jnp.float32)

@jax.custom_vjp
def low_back(v):
    return v

def low_keep(v):
    return (low(v), None)

def low_pass(kept, grad):
    return (grad,)

def back_keep(v):
    return (v, None)

def back_low(kept, grad):
    return (low(grad),)
low.defvjp(low_keep, low_pass)
low_back.defvjp(back_keep, back_low)
EPSILON = 1e-06
THETA = 500000.0

def exact_dot(former, latter):
    return jnp.dot(former, latter, precision=lax.Precision.HIGHEST)

def rms_scale(values, gain_row):
    return values * lax.rsqrt(lax.optimization_barrier(jnp.mean(values * values, axis=-1, keepdims=True)) + EPSILON) * gain_row

def rotate_half(values):
    half_size = values.shape[-1] // 2
    return jnp.concatenate([-values[..., half_size:], values[..., :half_size]], axis=-1)

def rope_tables(places_pos, head_size):
    exponent = jnp.arange(0, head_size // 2, dtype=jnp.float32) * (2.0 / head_size)
    frequency = THETA ** (-exponent)
    angles = places_pos.astype(jnp.float32)[:, None] * frequency[None, :]
    angles = jnp.concatenate([angles, angles], axis=-1)
    return (jnp.cos(angles), jnp.sin(angles))

def apply_rotary(values, cosine, sine_table):
    return values * cosine[:, None, :] + rotate_half(values) * sine_table[:, None, :]

def attend(queries, keys_all, values_all, starts):
    seq_count = queries.shape[0]
    head_count = queries.shape[1]
    head_size = queries.shape[2]
    block_rows = min(512, seq_count)
    blocks = seq_count // block_rows
    places = jnp.arange(seq_count, dtype=jnp.int32)
    factor = head_size ** (-0.5)

    def one_block(packed):
        query_block, place_block, start_block = packed
        scores = jnp.einsum('qhd,khd->hqk', query_block, keys_all, precision=lax.Precision.HIGHEST)
        scores = low_back(scores * factor)
        visible = (places[None, :] <= place_block[:, None]) & (starts[None, :] == start_block[:, None])
        scores = jnp.where(visible[None], scores, -1e+30)
        maximum = lax.optimization_barrier(jnp.max(scores, axis=-1, keepdims=True))
        expo_vals = jnp.exp(scores - maximum)
        soft_weights = low(expo_vals / lax.optimization_barrier(jnp.sum(expo_vals, axis=-1, keepdims=True)))
        return jnp.einsum('hqk,khd->qhd', soft_weights, values_all, precision=lax.Precision.HIGHEST)
    outcome = lax.map(jax.checkpoint(one_block), (queries.reshape(blocks, block_rows, head_count, head_size), places.reshape(blocks, block_rows), starts.reshape(blocks, block_rows)))
    return outcome.reshape(seq_count, head_count, head_size)

def layer(params, inputs, cosine, sine_table, starts):
    q_weight, k_weight, v_weight, o_weight, q_gain, k_gain, a_gain, g_weight, u_weight, d_weight, m_gain = params
    seq_count = inputs.shape[0]
    shaped = (seq_count, HEADS, HEAD_DIM)
    q_proj = low_back(exact_dot(inputs, q_weight))
    k_proj = low_back(exact_dot(inputs, k_weight))
    v_proj = low_back(low(exact_dot(inputs, v_weight)))
    q_rot = low_back(low(apply_rotary(rms_scale(q_proj, q_gain).reshape(shaped), cosine, sine_table)))
    k_rot = low_back(low(apply_rotary(rms_scale(k_proj, k_gain).reshape(shaped), cosine, sine_table)))
    attended = attend(q_rot, k_rot, v_proj.reshape(shaped), starts).reshape(seq_count, -1)
    attended = low_back(low(attended))
    a_proj = low_back(exact_dot(attended, o_weight))
    hidden = inputs + rms_scale(a_proj, a_gain)
    hidden_low = low(hidden)
    gate_proj = low_back(exact_dot(hidden_low, g_weight))
    up_proj = low_back(exact_dot(hidden_low, u_weight))
    activated = low(gate_proj * jax.nn.sigmoid(gate_proj) * up_proj)
    m_proj = low_back(exact_dot(activated, d_weight))
    return hidden + rms_scale(m_proj, m_gain)

def reference(tokens, positions, out_grad, w_query, w_key, w_value, w_output, query_gain, key_gain, attn_gain, w_gate, w_up, w_down, mlp_gain):
    params = tuple((tensor.astype(jnp.float32) for tensor in (w_query, w_key, w_value, w_output, query_gain, key_gain, attn_gain, w_gate, w_up, w_down, mlp_gain)))
    seq_count = tokens.shape[2]
    feature_count = tokens.shape[3]
    flat_tokens = tokens.reshape(-1, seq_count, feature_count).astype(jnp.float32)
    flat_grads = out_grad.reshape(-1, seq_count, feature_count).astype(jnp.float32)
    flat_pos = positions.reshape(-1, seq_count).astype(jnp.int32)
    initial = tuple((jnp.zeros_like(tensor) for tensor in params))

    def one_sequence(totals, packed):
        inputs, incoming, places_pos = packed
        cosine, sine_table = rope_tables(places_pos, HEAD_DIM)
        starts = jnp.arange(seq_count, dtype=jnp.int32) - places_pos

        def forward(weights_all, inputs_now):
            return layer(weights_all, inputs_now, cosine, sine_table, starts)
        result, pullback = jax.vjp(forward, params, inputs)
        weight_grads, input_grads = pullback(incoming)
        totals = tuple((total_now + grad_now for total_now, grad_now in zip(totals, weight_grads)))
        return (totals, (result.astype(jnp.bfloat16), input_grads.astype(jnp.bfloat16)))
    totals, (mixed, input_grad) = lax.scan(one_sequence, initial, (flat_tokens, flat_grads, flat_pos))
    return (mixed.reshape(tokens.shape), input_grad.reshape(tokens.shape), totals[0], totals[1], totals[2], totals[3], totals[4], totals[5], totals[6], totals[7], totals[8], totals[9], totals[10])
```

```python
import functools

import jax
import jax.numpy as jnp
from jax import lax
from jax.experimental import pallas as pl
from jax.experimental.pallas import tpu as pltpu
from jax.sharding import PartitionSpec as P

HEADS = 16
HEAD_DIM = 128

EPSILON = 1e-06
THETA = 500000.0

BF16 = jnp.bfloat16
F32 = jnp.float32
BOTH = ("fsdp", "seq")

GROUP = 4

UNREAD = pl.BlockSpec(memory_space=pl.ANY)
NO_COST = pl.CostEstimate(flops=0, bytes_accessed=0, transcendentals=0)


def cost(flops):
    return pl.CostEstimate(flops=int(flops * 1), bytes_accessed=0, transcendentals=0)


def dot_nn(former, latter):
    return jnp.dot(former, latter, preferred_element_type=F32)


def dot_tn(former, latter):
    return lax.dot_general(former, latter, (((0,), (0,)), ((), ())), preferred_element_type=F32)


def dot_nt(former, latter):
    return lax.dot_general(former, latter, (((1,), (1,)), ((), ())), preferred_element_type=F32)


def inv_rms(values):
    return lax.rsqrt(jnp.mean(values * values, axis=-1, keepdims=True) + EPSILON)


def norm_back(incoming, values, factor, gain_row):
    weighted = incoming * gain_row
    inner_mean = jnp.mean(weighted * values, axis=-1, keepdims=True)
    result_grad = factor * (weighted - values * factor * factor * inner_mean)
    return (result_grad, jnp.sum(incoming * values * factor, axis=0))


def rope_tables(places_pos):
    half = HEAD_DIM // 2
    exponent = jnp.arange(0, half, dtype=F32) * (2.0 / HEAD_DIM)
    frequency = THETA ** (-exponent)
    angles = places_pos.astype(F32)[:, None] * frequency[None, :]
    cosine, sine = jnp.cos(angles), jnp.sin(angles)
    return (
        jnp.concatenate([cosine, cosine], axis=-1),
        jnp.concatenate([-sine, sine], axis=-1),
    )


def bits_of(size):
    return [1 << i for i in range(size.bit_length() - 1)]


def exchange(values, axis, bit):
    return lax.ppermute(values, axis, [(i, i ^ bit) for i in range(lax.axis_size(axis))])


def sum_small(values, axis):
    for bit in bits_of(lax.axis_size(axis)):
        values = values + exchange(values, axis, bit)
    return values


def after(values, *earlier):
    return pl.pallas_call(
        lambda *refs: None,
        in_specs=[UNREAD] * (1 + len(earlier)),
        out_specs=UNREAD,
        out_shape=jax.ShapeDtypeStruct(values.shape, values.dtype),
        input_output_aliases={0: 0},
        cost_estimate=NO_COST,
    )(values, *earlier)


def gather_group(values):
    near, far = 1, 2
    other = exchange(values, "seq", far)
    return jnp.concatenate(
        [values, other, exchange(values, "seq", near), exchange(other, "seq", near)]
    )


def halve(held, bits, axis, stride=1):
    for i, bit in enumerate(bits):
        sent = {m: exchange(v, axis, bit * stride) for m, v in held.items() if m & bit}
        held = {m: held[m].astype(F32) + sent[m ^ bit].astype(F32) for m in held if not m & bit}
        if i < len(bits) - 1:
            held = {m: v.astype(BF16) for m, v in held.items()}
    return held[0]


def scatter_near(values):
    rows = values.shape[0] // 2
    return values[:rows].astype(F32) + exchange(values[rows:], "seq", 1).astype(F32)


def scatter_far(half, *earlier):
    rows = half.shape[0] // 2
    return half[:rows] + after(exchange(half[rows:].astype(BF16), "seq", 2), *earlier).astype(F32)


def gather_outer(values):
    groups = lax.axis_size("seq") // GROUP
    own = lax.axis_index("seq") // GROUP
    found = {0: values}
    for bit in bits_of(groups):
        found |= {m ^ bit: exchange(v, "seq", bit * GROUP) for m, v in found.items()}
    blocks = []
    for i in range(groups):
        block = found[0]
        for m in range(1, groups):
            block = jnp.where((own ^ i) == m, found[m], block)
        blocks.append(block)
    return jnp.concatenate(blocks)


def scatter_outer(values):
    groups = lax.axis_size("seq") // GROUP
    own = lax.axis_index("seq") // GROUP
    rows = values.shape[0] // groups
    held = {
        m: lax.dynamic_slice_in_dim(values, (own ^ m) * rows, rows, 0) for m in range(groups)
    }
    return halve(held, bits_of(groups)[::-1], "seq", GROUP)


def shift(values, step):
    size = lax.axis_size("seq")
    pairs = [(i, i + 2 * step) for i in range(size) if 0 <= i + 2 * step < size]
    return lax.ppermute(values, "seq", pairs)


def scatter_line(values, *earlier):
    size, place = lax.axis_size("seq"), lax.axis_index("seq")
    pairs, pair, core = size // 2, place // 2, place % 2
    rows = values.shape[0] // size
    blocks = values.reshape(pairs, 2, rows, values.shape[1])
    sent = exchange(lax.dynamic_index_in_dim(blocks, 1 - core, 1, keepdims=False), "seq", 1)
    kept = lax.dynamic_index_in_dim(blocks, core, 1, keepdims=False)
    blocks = (kept.astype(F32) + sent.astype(F32)).astype(BF16)
    total = lax.dynamic_index_in_dim(blocks, pair, 0, keepdims=False).astype(F32)
    for step in (1, -1):
        moving = None
        for far in range(pairs - 1, 0, -1):
            target = jnp.clip(pair + step * far, 0, pairs - 1)
            block = lax.dynamic_index_in_dim(blocks, target, 0, keepdims=False)
            if moving is not None:
                block = (block.astype(F32) + moving.astype(F32)).astype(BF16)
            moving = shift(block, step)
        total = total + after(moving, *earlier).astype(F32)
    return total


def gather_placed(values, axis):
    size, own = lax.axis_size(axis), lax.axis_index(axis)
    bits, rows = bits_of(size), values.shape[0]
    parts = [(0, values, bits[::-1])]
    if axis == "fsdp":
        half = rows // 2
        parts = [(0, values[:half], bits), (half, values[half:], bits[::-1])]
    out = jnp.zeros((size * rows, values.shape[1]), values.dtype)
    for first, part, order in parts:
        found = {0: part}
        for bit in order:
            found |= {m ^ bit: exchange(v, axis, bit) for m, v in found.items()}
        for m, v in found.items():
            out = lax.dynamic_update_slice_in_dim(out, v, (own ^ m) * rows + first, 0)
    return out


def ordered(kernel, count, earlier):
    return lambda *refs: kernel(*refs[:count], *refs[count + len(earlier) :])


def gate_up_kernel(rows_ref, gate_ref, up_ref, gate_out, up_out, act_out):
    gate = dot_nn(rows_ref[...], gate_ref[...])
    up = dot_nn(rows_ref[...], up_ref[...])
    gate_out[...] = gate.astype(BF16)
    up_out[...] = up.astype(BF16)
    act_out[...] = (gate * jax.nn.sigmoid(gate) * up).astype(BF16)


def down_kernel(act_ref, down_ref, out_ref):
    out_ref[...] = dot_nn(act_ref[...], down_ref[...]).astype(BF16)


def act_back_kernel(grad_ref, down_ref, gate_ref, up_ref, dgate_ref, dup_ref):
    dact = dot_nt(grad_ref[...], down_ref[...])
    gate, up = gate_ref[...].astype(F32), up_ref[...].astype(F32)
    sigmoid = jax.nn.sigmoid(gate)
    dgate_ref[...] = (dact * up * sigmoid * (1.0 + gate * (1.0 - sigmoid))).astype(BF16)
    dup_ref[...] = (dact * gate * sigmoid).astype(BF16)


def hidden_back_kernel(dgate_ref, gate_ref, dup_ref, up_ref, out_ref):
    total = dot_nt(dgate_ref[...], gate_ref[...]) + dot_nt(dup_ref[...], up_ref[...])
    out_ref[...] = total.astype(BF16)


def weight_kernel(former_ref, latter_ref, out_ref):
    out_ref[...] = dot_tn(former_ref[...], latter_ref[...]).astype(BF16)


def held_rows(values):
    return pl.BlockSpec((min(1024, values.shape[0]), values.shape[1]), lambda j, i: (i, 0))


def cols_of(values, block):
    return pl.BlockSpec((values.shape[0], block), lambda j, i: (0, j))


def rows_of(values, block):
    return pl.BlockSpec((block, values.shape[1]), lambda j, i: (j, 0))


def tiles_of(values, block):
    return pl.BlockSpec((min(1024, values.shape[0]), block), lambda j, i: (i, j))


def by_columns(kernel, operands, specs, outs, cols, earlier, products=1):
    rows = operands[0].shape[0]
    high = min(1024, rows)
    return pl.pallas_call(
        ordered(kernel, len(operands), earlier),
        grid=(cols // 512, rows // high),
        in_specs=specs + [UNREAD] * len(earlier),
        out_specs=[pl.BlockSpec((high, 512), lambda j, i: (i, j))] * outs,
        out_shape=[jax.ShapeDtypeStruct((rows, cols), BF16)] * outs,
        compiler_params=pltpu.CompilerParams(vmem_limit_bytes=56 << 20),
        cost_estimate=cost(products * rows * cols * operands[0].shape[1] * 2),
    )(*operands, *earlier)


def gate_up(rows, gate, up, *earlier):
    specs = [held_rows(rows), cols_of(gate, 512), cols_of(up, 512)]
    return by_columns(gate_up_kernel, (rows, gate, up), specs, 3, gate.shape[1], earlier, 2)


def down(act, weight, *earlier):
    specs = [held_rows(act), cols_of(weight, 512)]
    return by_columns(down_kernel, (act, weight), specs, 1, weight.shape[1], earlier)[0]


def act_back(grads, weight, gate, up, *earlier):
    specs = [held_rows(grads), rows_of(weight, 512), tiles_of(gate, 512), tiles_of(up, 512)]
    return by_columns(act_back_kernel, (grads, weight, gate, up), specs, 2, gate.shape[1], earlier)


def hidden_back(dgate, gate, dup, up, *earlier):
    specs = [held_rows(dgate), rows_of(gate, 512), held_rows(dup), rows_of(up, 512)]
    return by_columns(hidden_back_kernel, (dgate, gate, dup, up), specs, 1, gate.shape[0], earlier, 2)[0]


def weight_grad(former, latter, *earlier):
    rows, cols = former.shape[1], latter.shape[1]
    block = min(512, rows)
    specs = [
        pl.BlockSpec((former.shape[0], block), lambda j: (0, j)),
        pl.BlockSpec(latter.shape, lambda j: (0, 0)),
    ]
    return pl.pallas_call(
        ordered(weight_kernel, 2, earlier),
        grid=(rows // block,),
        in_specs=specs + [UNREAD] * len(earlier),
        out_specs=pl.BlockSpec((block, cols), lambda j: (j, 0)),
        out_shape=jax.ShapeDtypeStruct((rows, cols), BF16),
        compiler_params=pltpu.CompilerParams(vmem_limit_bytes=56 << 20),
        cost_estimate=cost(former.shape[0] * rows * cols * 2),
    )(former, latter, *earlier)


def project_kernel(rows_ref, weight_ref, out_ref, squares_ref):
    width = weight_ref.shape[1] // 3
    proj = dot_nn(rows_ref[...], weight_ref[...])
    out_ref[...] = proj
    squares = (proj[:, : 2 * width] * proj[:, : 2 * width]).astype(BF16)
    part = lax.broadcasted_iota(jnp.int32, (8, 2 * width), 1) // width
    chosen = part == lax.broadcasted_iota(jnp.int32, (8, 2 * width), 0)
    squares_ref[...] = dot_nt(chosen.astype(BF16), squares)


def project(rows, weight):
    count, depth = rows.shape
    block = min(512, count)
    cols = weight.shape[1]
    return pl.pallas_call(
        project_kernel,
        grid=(count // block,),
        in_specs=[
            pl.BlockSpec((block, depth), lambda i: (i, 0)),
            pl.BlockSpec(weight.shape, lambda i: (0, 0)),
        ],
        out_specs=[
            pl.BlockSpec((block, cols), lambda i: (i, 0)),
            pl.BlockSpec((8, block), lambda i: (0, i)),
        ],
        out_shape=[
            jax.ShapeDtypeStruct((count, cols), F32),
            jax.ShapeDtypeStruct((8, count), F32),
        ],
        compiler_params=pltpu.CompilerParams(vmem_limit_bytes=48 << 20),
        cost_estimate=cost(count * depth * cols * 2),
    )(rows, weight)


def prepare_kernel(proj_ref, scale_ref, gain_ref, cos_ref, sin_ref, q_ref, k_ref, v_ref):
    width = q_ref.shape[1]
    cosine, sine = cos_ref[...], sin_ref[...]
    for part, out_ref in ((0, q_ref), (1, k_ref)):
        scale = scale_ref[:, part : part + 1]
        for low in range(0, width, HEAD_DIM):
            cols = slice(part * width + low, part * width + low + HEAD_DIM)
            normed = proj_ref[:, cols] * scale * gain_ref[:, cols]
            turned = normed * cosine + pltpu.roll(normed, HEAD_DIM // 2, 1) * sine
            out_ref[:, low : low + HEAD_DIM] = turned.astype(BF16)
    v_ref[...] = proj_ref[:, 2 * width :].astype(BF16)


def prepare(proj, scales, gains, cosine, sine):
    rows, width3 = proj.shape
    width = width3 // 3
    block = min(512, rows)
    by_rows = lambda cols: pl.BlockSpec((block, cols), lambda i: (i, 0))
    return pl.pallas_call(
        prepare_kernel,
        grid=(rows // block,),
        in_specs=[
            by_rows(width3),
            by_rows(2),
            pl.BlockSpec((1, 2 * width), lambda i: (0, 0)),
            by_rows(HEAD_DIM),
            by_rows(HEAD_DIM),
        ],
        out_specs=[by_rows(width)] * 3,
        out_shape=[jax.ShapeDtypeStruct((rows, width), BF16)] * 3,
        cost_estimate=cost(rows * width3 * 3600),
    )(proj, scales, gains, cosine, sine)


def unprepare_kernel(
    dq_ref, dk_ref, dv_ref, proj_ref, scale_ref, inner_ref, gain_ref, cos_ref, sin_ref, out_ref, sum_ref
):
    width = dq_ref.shape[1]

    @pl.when(pl.program_id(0) == 0)
    def _():
        sum_ref[...] = jnp.zeros_like(sum_ref)

    cosine, sine = cos_ref[...], sin_ref[...]
    for part, in_ref in ((0, dq_ref), (1, dk_ref)):
        scale = scale_ref[:, part : part + 1]
        inner = inner_ref[:, part : part + 1]
        for low in range(0, width, HEAD_DIM):
            cols = slice(part * width + low, part * width + low + HEAD_DIM)
            turned = in_ref[:, low : low + HEAD_DIM].astype(F32)
            normed = turned * cosine - pltpu.roll(turned, HEAD_DIM // 2, 1) * sine
            scaled = proj_ref[:, cols] * scale
            sum_ref[:, cols] += jnp.sum(normed * scaled, axis=0, keepdims=True)
            result = scale * (normed * gain_ref[:, cols] - scaled * inner)
            out_ref[:, cols] = result.astype(BF16)
    out_ref[:, 2 * width :] = dv_ref[...]


def unprepare(dq, dk, dv, proj, scales, inner, gains, cosine, sine):
    rows, width3 = proj.shape
    width = width3 // 3
    block = min(512, rows)
    by_rows = lambda cols: pl.BlockSpec((block, cols), lambda i: (i, 0))
    fixed = pl.BlockSpec((1, 2 * width), lambda i: (0, 0))
    return pl.pallas_call(
        unprepare_kernel,
        grid=(rows // block,),
        in_specs=[by_rows(width)] * 3
        + [by_rows(width3), by_rows(2), by_rows(2), fixed, by_rows(HEAD_DIM), by_rows(HEAD_DIM)],
        out_specs=[by_rows(width3), fixed],
        out_shape=[
            jax.ShapeDtypeStruct((rows, width3), BF16),
            jax.ShapeDtypeStruct((1, 2 * width), F32),
        ],
        cost_estimate=cost(rows * width3 * 4700),
    )(dq, dk, dv, proj, scales, inner, gains, cosine, sine)


def visible_mask(first, keys, rows, starts):
    key_ids = lax.broadcasted_iota(jnp.int32, (keys, rows), 0)
    query_ids = first + lax.broadcasted_iota(jnp.int32, (keys, rows), 1)
    return (key_ids <= query_ids) & (key_ids >= starts)


def forward_kernel(q_ref, k_ref, v_ref, start_ref, o_ref, lse_ref, *, factor, blocks):
    block = lse_ref.shape[-1]
    whole = blocks * block
    for turn in range(blocks):

        @pl.when(pl.program_id(2) == turn)
        def _():
            keys = (turn + 1) * block
            queries = q_ref[...].reshape(block, HEAD_DIM)
            keys_all = k_ref[...].reshape(whole, HEAD_DIM)[:keys]
            values = v_ref[...].reshape(whole, HEAD_DIM)[:keys]
            scores = dot_nt(keys_all, queries) * factor
            visible = visible_mask(turn * block, keys, block, start_ref[0])
            scores = jnp.where(visible, scores, -1e30)
            top = jnp.max(scores, axis=0, keepdims=True)
            expo = jnp.exp(scores - top)
            total = jnp.sum(expo, axis=0, keepdims=True)
            outcome = dot_tn(values, expo.astype(BF16)) / total
            o_ref[...] = outcome.T.astype(BF16).reshape(o_ref.shape)
            lse_ref[0, 0] = top + jnp.log(total)


def backward_kernel(
    q_ref, k_ref, v_ref, start_ref, do_ref, lse_ref, dq_ref, dk_ref, dv_ref, dk_sum, dv_sum, *, factor, blocks
):
    block = lse_ref.shape[-1]
    whole = blocks * block

    @pl.when(pl.program_id(2) == 0)
    def _():
        dk_sum[...] = jnp.zeros_like(dk_sum)
        dv_sum[...] = jnp.zeros_like(dv_sum)

    for turn in range(blocks):

        @pl.when(pl.program_id(2) == turn)
        def _():
            keys = (turn + 1) * block
            queries = q_ref[...].reshape(block, HEAD_DIM)
            grads = do_ref[...].reshape(block, HEAD_DIM)
            keys_all = k_ref[...].reshape(whole, HEAD_DIM)[:keys]
            values = v_ref[...].reshape(whole, HEAD_DIM)[:keys]
            scores = dot_nt(keys_all, queries) * factor
            visible = visible_mask(turn * block, keys, block, start_ref[0])
            soft = jnp.where(visible, jnp.exp(scores - lse_ref[0, 0]), 0.0)
            dv_sum[:keys] += dot_nn(soft.astype(BF16), grads)
            dsoft = dot_nt(values, grads)
            delta = jnp.sum(dsoft * soft, axis=0, keepdims=True)
            dscores = (soft * (dsoft - delta)).astype(BF16)
            dk_sum[:keys] += dot_nn(dscores, queries)
            dq = dot_tn(keys_all, dscores) * factor
            dq_ref[...] = dq.T.astype(BF16).reshape(dq_ref.shape)

    @pl.when(pl.program_id(2) == blocks - 1)
    def _():
        dk_ref[...] = (dk_sum[...] * factor).astype(BF16).reshape(dk_ref.shape)
        dv_ref[...] = dv_sum[...].astype(BF16).reshape(dv_ref.shape)


def attention_specs(shape):
    groups, count, rows, width = shape
    whole = groups * rows
    block = min(512, whole)
    per = block // rows
    some = pl.BlockSpec((per, 1, rows, HEAD_DIM), lambda b, h, i: (i, b, 0, h))
    every = pl.BlockSpec((groups, 1, rows, HEAD_DIM), lambda b, h, i: (0, b, 0, h))
    starts = pl.BlockSpec((1, 1, block), lambda b, h, i: (b, 0, i))
    sums = pl.BlockSpec((1, 1, 1, block), lambda b, h, i: (b, h, 0, i))
    heads = width // HEAD_DIM
    pairs = count * heads * whole * whole
    return some, every, starts, sums, (count, heads, whole // block), whole, pairs


def attend_forward(queries, keys, values, starts, factor, *earlier):
    some, every, start_spec, sums, grid, whole, pairs = attention_specs(queries.shape)
    return pl.pallas_call(
        ordered(functools.partial(forward_kernel, factor=factor, blocks=grid[2]), 4, earlier),
        grid=grid,
        in_specs=[some, every, every, start_spec] + [UNREAD] * len(earlier),
        out_specs=[some, sums],
        out_shape=[
            jax.ShapeDtypeStruct(queries.shape, BF16),
            jax.ShapeDtypeStruct((grid[0], grid[1], 1, whole), F32),
        ],
        compiler_params=pltpu.CompilerParams(vmem_limit_bytes=48 << 20),
        cost_estimate=cost(pairs * HEAD_DIM * 11),
    )(queries, keys, values, starts, *earlier)


def attend_backward(queries, keys, values, starts, grads, log_sums, factor, *earlier):
    some, every, start_spec, sums, grid, whole, pairs = attention_specs(queries.shape)
    return pl.pallas_call(
        ordered(functools.partial(backward_kernel, factor=factor, blocks=grid[2]), 6, earlier),
        grid=grid,
        in_specs=[some, every, every, start_spec, some, sums] + [UNREAD] * len(earlier),
        out_specs=[some, every, every],
        out_shape=[jax.ShapeDtypeStruct(queries.shape, BF16)] * 3,
        scratch_shapes=[pltpu.VMEM((whole, HEAD_DIM), F32)] * 2,
        compiler_params=pltpu.CompilerParams(vmem_limit_bytes=52 << 20),
        cost_estimate=cost(pairs * HEAD_DIM * 20),
    )(queries, keys, values, starts, grads, log_sums, *earlier)


def on_device(
    tokens,
    positions,
    out_grad,
    w_query,
    w_key,
    w_value,
    w_output,
    query_gain,
    key_gain,
    attn_gain,
    w_gate,
    w_up,
    w_down,
    mlp_gain,
):
    fsdp, seq = lax.axis_size("fsdp"), lax.axis_size("seq")
    row, place = lax.axis_index("fsdp"), lax.axis_index("seq")
    groups = seq // GROUP
    factor = HEAD_DIM ** (-0.5)
    count = tokens.shape[0] * tokens.shape[1]
    tok_count, width = tokens.shape[2], tokens.shape[3]
    own_rows = count * tok_count
    local_width = width // seq
    hidden_width = w_gate.shape[1] // GROUP
    share = w_query.shape[0]
    down_share = w_down.shape[0]
    head_shape = (seq, count, tok_count, local_width)

    inputs = tokens.reshape(own_rows, width)
    grad_rows = out_grad.reshape(own_rows, width).astype(F32)
    inputs_all = lax.all_gather(inputs, "seq", axis=0, tiled=True)

    qkv_weight = lax.all_to_all(
        jnp.stack([w_query, w_key, w_value]), "seq", split_axis=2, concat_axis=1, tiled=True
    )
    qkv_weight = jnp.moveaxis(qkv_weight, 0, 1).reshape(seq * share, 3 * local_width)
    qkv_weight = gather_placed(qkv_weight, "fsdp")

    own_gains = jnp.stack([query_gain, key_gain, attn_gain, mlp_gain]).astype(F32)
    small = jnp.concatenate([own_gains.reshape(-1), positions.reshape(-1).astype(F32)])
    small = lax.dynamic_update_index_in_dim(jnp.zeros((seq, small.shape[0]), F32), small, place, 0)
    small = sum_small(small, "seq")
    gains = small[:, : 4 * share].reshape(seq, 4, share)
    gains = lax.dynamic_update_index_in_dim(jnp.zeros((fsdp, seq, 4, share), F32), gains, row, 0)
    gains = jnp.moveaxis(sum_small(gains, "fsdp"), 2, 0).reshape(4, 1, width)
    a_gain, m_gain = gains[2], gains[3]
    qk_gain = lax.dynamic_slice_in_dim(gains[:2], place * local_width, local_width, 2)
    qk_gain = qk_gain.reshape(1, 2 * local_width)
    places = small[:, 4 * share :].reshape(seq, count, tok_count)
    cosine, sine = rope_tables(places.reshape(-1))
    order = jnp.arange(seq * tok_count, dtype=jnp.int32).reshape(seq, 1, tok_count)
    starts = jnp.moveaxis(order - places.astype(jnp.int32), 0, 1).reshape(count, 1, seq * tok_count)

    def columns(weight):
        part = weight.reshape(share, fsdp * groups, GROUP, down_share)
        part = jnp.moveaxis(part, 2, 0).reshape(1, GROUP, share, hidden_width)
        part = jnp.broadcast_to(part, (groups, GROUP, share, hidden_width))
        part = part.reshape(seq * share, hidden_width)
        return lax.all_to_all(part, "seq", split_axis=0, concat_axis=0, tiled=True)

    inputs_all = after(inputs_all, qkv_weight, cosine, sine, starts, gains)
    g_part = columns(after(w_gate, inputs_all))
    o_weight = lax.all_gather(w_output, BOTH, axis=0, tiled=True)
    proj, squares = project(inputs_all, qkv_weight)
    scales = lax.rsqrt(sum_small(squares[:2], "seq") / width + EPSILON).T
    rotated = prepare(proj, scales, qk_gain, cosine, sine)
    g_part = after(g_part, *rotated)
    u_part = columns(after(w_up, g_part))
    g_weight = lax.all_gather(g_part, "fsdp", axis=0, tiled=True)
    rotated = [v.reshape(head_shape) for v in rotated]
    attended, log_sums = attend_forward(*rotated, starts, factor)
    attended = after(attended, u_part)
    attn_rows = lax.all_to_all(
        attended.reshape(seq, own_rows, local_width), "seq", split_axis=0, concat_axis=0, tiled=True
    )
    attn_rows = jnp.moveaxis(attn_rows, 0, 1).reshape(own_rows, width)

    a_proj = dot_nn(attn_rows, o_weight)
    a_scale = inv_rms(a_proj)
    hidden = inputs.astype(F32) + a_proj * a_scale * a_gain
    d_part = gather_outer(after(w_down, u_part))
    u_weight, d_weight = (lax.all_gather(v, "fsdp", axis=0, tiled=True) for v in (u_part, d_part))
    hidden_low = gather_group(hidden.astype(BF16))
    gate, up, act = gate_up(hidden_low, g_weight, u_weight)
    m_proj = scatter_far(scatter_near(down(act, d_weight)))
    m_scale = inv_rms(m_proj)
    mixed = (hidden + m_proj * m_scale * m_gain).astype(BF16)

    grad_mproj, grad_mgain = norm_back(grad_rows, m_proj, m_scale, m_gain)
    grad_mproj = gather_group(grad_mproj.astype(BF16))

    def over_rows(part):
        return lax.psum_scatter(part, "fsdp", scatter_dimension=0, tiled=True)

    def columns_back(part):
        part = lax.all_to_all(part, "seq", split_axis=0, concat_axis=0, tiled=True).astype(F32)
        part = part.reshape(groups, GROUP, share, fsdp * groups, down_share).sum(axis=0)
        return jnp.moveaxis(part, 0, 2).reshape(share, -1)

    dgate, dup = act_back(grad_mproj, d_weight, gate, up)
    down_grad = weight_grad(act, grad_mproj, dgate)
    share_down = over_rows(down_grad)
    grads = hidden_back(dgate, g_weight, dup, u_weight, down_grad)
    gate_grad = weight_grad(hidden_low, dgate, grads)
    share_gate = over_rows(gate_grad)
    grads = scatter_near(grads)
    up_grad = weight_grad(hidden_low, dup, gate_grad, grads)
    share_up = over_rows(up_grad)
    grad_hidden = grad_rows + scatter_far(grads, up_grad)

    grad_aproj, grad_again = norm_back(grad_hidden, a_proj, a_scale, a_gain)
    grad_aproj = grad_aproj.astype(BF16)
    grad_attn = dot_nt(grad_aproj, o_weight).astype(BF16)
    grad_attn = jnp.moveaxis(grad_attn.reshape(own_rows, seq, local_width), 1, 0)
    grad_heads = lax.all_to_all(grad_attn, "seq", split_axis=0, concat_axis=0, tiled=True)
    o_grad = weight_grad(attn_rows, grad_aproj, grad_attn)
    share_output = over_rows(o_grad)
    grad_heads = after(grad_heads, o_grad)
    share_down = scatter_outer(after(share_down, grad_heads))
    dq, dk, dv = attend_backward(
        *rotated, starts, grad_heads.reshape(head_shape), log_sums, factor
    )
    dq = after(dq, share_down)
    dq, dk, dv = (v.reshape(seq * own_rows, local_width) for v in (dq, dk, dv))
    q_rot, k_rot = (v.reshape(seq * own_rows, local_width) for v in rotated[:2])
    inner = jnp.stack(
        [
            jnp.sum(dq.astype(F32) * q_rot.astype(F32), axis=1),
            jnp.sum(dk.astype(F32) * k_rot.astype(F32), axis=1),
        ]
    )
    inner = sum_small(inner, "seq") / width
    grad_qkv, gain_sums = unprepare(
        dq, dk, dv, proj, scales, inner.T, qk_gain, cosine, sine
    )
    partial = dot_nt(grad_qkv, qkv_weight).astype(BF16)
    qkv_grad = weight_grad(inputs_all, grad_qkv, partial)
    share_output = lax.psum_scatter(share_output, "seq", scatter_dimension=0, tiled=True).astype(F32)
    qkv_grad = after(qkv_grad, share_output)
    share_gate = columns_back(after(share_gate, grad_qkv))
    share_up = columns_back(after(share_up, grad_qkv))
    share_qkv = over_rows(qkv_grad)
    share_qkv = lax.all_to_all(
        share_qkv.reshape(seq, share, 3 * local_width), "seq", split_axis=0, concat_axis=0, tiled=True
    )
    share_qkv = share_qkv.reshape(seq, share, 3, local_width).transpose(2, 1, 0, 3)
    share_qkv = share_qkv.reshape(3, share, width).astype(F32)
    slots = lax.dynamic_update_slice_in_dim(
        jnp.zeros((2, width), F32), gain_sums.reshape(2, local_width), place * local_width, 1
    )
    slots = jnp.concatenate([slots, grad_again[None], grad_mgain[None]])
    slots = sum_small(sum_small(slots, "fsdp"), "seq")
    gain_grads = lax.dynamic_slice_in_dim(slots, (row * seq + place) * share, share, 1)
    grad_inputs = scatter_line(partial, share_gate, share_up, share_qkv, gain_grads)
    input_grad = (grad_hidden + grad_inputs).astype(BF16)
    return (
        mixed.reshape(tokens.shape),
        input_grad.reshape(tokens.shape),
        share_qkv[0],
        share_qkv[1],
        share_qkv[2],
        share_output,
        gain_grads[0],
        gain_grads[1],
        gain_grads[2],
        share_gate,
        share_up,
        share_down,
        gain_grads[3],
    )


def solution(mesh):
    rows = P(BOTH, None)
    flat = P(BOTH)
    acts = P(None, "fsdp", "seq", None)
    return jax.shard_map(
        on_device,
        mesh=mesh,
        in_specs=(acts, P(None, "fsdp", "seq"), acts, rows, rows, rows, rows, flat, flat, flat)
        + (rows, rows, rows, flat),
        out_specs=(acts, acts, rows, rows, rows, rows, flat, flat, flat, rows, rows, rows, flat),
        check_vma=False,
    )
```

```python
import functools

import jax
import jax.numpy as jnp
from jax import lax
from jax.experimental import pallas as pl
from jax.experimental.pallas import tpu as pltpu
from jax.sharding import PartitionSpec as P

HEADS = 16
HEAD_DIM = 128

EPSILON = 1e-06
THETA = 500000.0

BF16 = jnp.bfloat16
F32 = jnp.float32
BOTH = ("fsdp", "seq")

GROUP = 4

UNREAD = pl.BlockSpec(memory_space=pl.ANY)
NO_COST = pl.CostEstimate(flops=0, bytes_accessed=0, transcendentals=0)


def cost(flops):
    return pl.CostEstimate(flops=int(flops * 1), bytes_accessed=0, transcendentals=0)


def dot_nn(former, latter):
    return jnp.dot(former, latter, preferred_element_type=F32)


def dot_tn(former, latter):
    return lax.dot_general(former, latter, (((0,), (0,)), ((), ())), preferred_element_type=F32)


def dot_nt(former, latter):
    return lax.dot_general(former, latter, (((1,), (1,)), ((), ())), preferred_element_type=F32)


def inv_rms(values):
    return lax.rsqrt(jnp.mean(values * values, axis=-1, keepdims=True) + EPSILON)


def norm_back(incoming, values, factor, gain_row):
    weighted = incoming * gain_row
    inner_mean = jnp.mean(weighted * values, axis=-1, keepdims=True)
    result_grad = factor * (weighted - values * factor * factor * inner_mean)
    return (result_grad, jnp.sum(incoming * values * factor, axis=0))


def rope_tables(places_pos):
    half = HEAD_DIM // 2
    exponent = jnp.arange(0, half, dtype=F32) * (2.0 / HEAD_DIM)
    frequency = THETA ** (-exponent)
    angles = places_pos.astype(F32)[:, None] * frequency[None, :]
    cosine, sine = jnp.cos(angles), jnp.sin(angles)
    return (
        jnp.concatenate([cosine, cosine], axis=-1),
        jnp.concatenate([-sine, sine], axis=-1),
    )


def bits_of(size):
    return [1 << i for i in range(size.bit_length() - 1)]


def exchange(values, axis, bit):
    return lax.ppermute(values, axis, [(i, i ^ bit) for i in range(lax.axis_size(axis))])


def sum_small(values, axis):
    for bit in bits_of(lax.axis_size(axis)):
        values = values + exchange(values, axis, bit)
    return values


def after(values, *earlier):
    return pl.pallas_call(
        lambda *refs: None,
        in_specs=[UNREAD] * (1 + len(earlier)),
        out_specs=UNREAD,
        out_shape=jax.ShapeDtypeStruct(values.shape, values.dtype),
        input_output_aliases={0: 0},
        cost_estimate=NO_COST,
    )(values, *earlier)


def gather_group(values):
    near, far = 1, 2
    other = exchange(values, "seq", far)
    return jnp.concatenate(
        [values, other, exchange(values, "seq", near), exchange(other, "seq", near)]
    )


def halve(held, bits, axis, stride=1):
    for i, bit in enumerate(bits):
        sent = {m: exchange(v, axis, bit * stride) for m, v in held.items() if m & bit}
        held = {m: held[m].astype(F32) + sent[m ^ bit].astype(F32) for m in held if not m & bit}
        if i < len(bits) - 1:
            held = {m: v.astype(BF16) for m, v in held.items()}
    return held[0]


def scatter_near(values):
    rows = values.shape[0] // 2
    return values[:rows].astype(F32) + exchange(values[rows:], "seq", 1).astype(F32)


def scatter_far(half, *earlier):
    rows = half.shape[0] // 2
    return half[:rows] + after(exchange(half[rows:].astype(BF16), "seq", 2), *earlier).astype(F32)


def gather_outer(values):
    groups = lax.axis_size("seq") // GROUP
    own = lax.axis_index("seq") // GROUP
    found = {0: values}
    for bit in bits_of(groups):
        found |= {m ^ bit: exchange(v, "seq", bit * GROUP) for m, v in found.items()}
    blocks = []
    for i in range(groups):
        block = found[0]
        for m in range(1, groups):
            block = jnp.where((own ^ i) == m, found[m], block)
        blocks.append(block)
    return jnp.concatenate(blocks)


def scatter_outer(values):
    groups = lax.axis_size("seq") // GROUP
    own = lax.axis_index("seq") // GROUP
    rows = values.shape[0] // groups
    held = {
        m: lax.dynamic_slice_in_dim(values, (own ^ m) * rows, rows, 0) for m in range(groups)
    }
    return halve(held, bits_of(groups)[::-1], "seq", GROUP)


def shift(values, step):
    size = lax.axis_size("seq")
    pairs = [(i, i + 2 * step) for i in range(size) if 0 <= i + 2 * step < size]
    return lax.ppermute(values, "seq", pairs)


def gather_placed(values, axis):
    size, own = lax.axis_size(axis), lax.axis_index(axis)
    bits, rows = bits_of(size), values.shape[0]
    parts = [(0, values, bits[::-1])]
    if axis == "fsdp":
        half = rows // 2
        parts = [(0, values[:half], bits), (half, values[half:], bits[::-1])]
    out = jnp.zeros((size * rows, values.shape[1]), values.dtype)
    for first, part, order in parts:
        found = {0: part}
        for bit in order:
            found |= {m ^ bit: exchange(v, axis, bit) for m, v in found.items()}
        for m, v in found.items():
            out = lax.dynamic_update_slice_in_dim(out, v, (own ^ m) * rows + first, 0)
    return out


def scatter_line(values, earlier):
    size, place = lax.axis_size("seq"), lax.axis_index("seq")
    pairs, pair, core = size // 2, place // 2, place % 2
    rows = values.shape[0] // size
    blocks = values.reshape(pairs, 2, rows, values.shape[1])
    sent = exchange(lax.dynamic_index_in_dim(blocks, 1 - core, 1, keepdims=False), "seq", 1)
    kept = lax.dynamic_index_in_dim(blocks, core, 1, keepdims=False)
    blocks = (kept.astype(F32) + sent.astype(F32)).astype(BF16)

    def block_at(place):
        place = jnp.clip(place, 0, pairs - 1)
        return lax.dynamic_index_in_dim(blocks, place, 0, keepdims=False)

    up = down = None
    for far in range(pairs - 1, 0, -1):
        next_up, next_down = block_at(pair + far), block_at(pair - far)
        if up is not None:
            next_up = (next_up.astype(F32) + up.astype(F32)).astype(BF16)
            next_down = (next_down.astype(F32) + down.astype(F32)).astype(BF16)
        up, down = shift(next_up, 1), shift(next_down, -1)
        up = after(up, down, *earlier.get(pairs - far, ()))
    return block_at(pair).astype(F32) + up.astype(F32) + down.astype(F32)


def ordered(kernel, count, earlier):
    return lambda *refs: kernel(*refs[:count], *refs[count + len(earlier) :])


def gate_up_kernel(rows_ref, gate_ref, up_ref, gate_out, up_out, act_out):
    gate = dot_nn(rows_ref[...], gate_ref[...])
    up = dot_nn(rows_ref[...], up_ref[...])
    gate_out[...] = gate.astype(BF16)
    up_out[...] = up.astype(BF16)
    act_out[...] = (gate * jax.nn.sigmoid(gate) * up).astype(BF16)


def down_kernel(act_ref, down_ref, out_ref):
    out_ref[...] = dot_nn(act_ref[...], down_ref[...]).astype(BF16)


def act_back_kernel(grad_ref, down_ref, gate_ref, up_ref, dgate_ref, dup_ref):
    dact = dot_nt(grad_ref[...], down_ref[...])
    gate, up = gate_ref[...].astype(F32), up_ref[...].astype(F32)
    sigmoid = jax.nn.sigmoid(gate)
    dgate_ref[...] = (dact * up * sigmoid * (1.0 + gate * (1.0 - sigmoid))).astype(BF16)
    dup_ref[...] = (dact * gate * sigmoid).astype(BF16)


def hidden_back_kernel(dgate_ref, gate_ref, dup_ref, up_ref, out_ref):
    total = dot_nt(dgate_ref[...], gate_ref[...]) + dot_nt(dup_ref[...], up_ref[...])
    out_ref[...] = total.astype(BF16)


def weight_kernel(former_ref, latter_ref, out_ref):
    out_ref[...] = dot_tn(former_ref[...], latter_ref[...]).astype(BF16)


def held_rows(values):
    return pl.BlockSpec((min(1024, values.shape[0]), values.shape[1]), lambda j, i: (i, 0))


def cols_of(values, block):
    return pl.BlockSpec((values.shape[0], block), lambda j, i: (0, j))


def rows_of(values, block):
    return pl.BlockSpec((block, values.shape[1]), lambda j, i: (j, 0))


def tiles_of(values, block):
    return pl.BlockSpec((min(1024, values.shape[0]), block), lambda j, i: (i, j))


def by_columns(kernel, operands, specs, outs, cols, earlier, products=1):
    rows = operands[0].shape[0]
    high = min(1024, rows)
    return pl.pallas_call(
        ordered(kernel, len(operands), earlier),
        grid=(cols // 512, rows // high),
        in_specs=specs + [UNREAD] * len(earlier),
        out_specs=[pl.BlockSpec((high, 512), lambda j, i: (i, j))] * outs,
        out_shape=[jax.ShapeDtypeStruct((rows, cols), BF16)] * outs,
        compiler_params=pltpu.CompilerParams(vmem_limit_bytes=56 << 20),
        cost_estimate=cost(products * rows * cols * operands[0].shape[1] * 2),
    )(*operands, *earlier)


def gate_up(rows, gate, up, *earlier):
    specs = [held_rows(rows), cols_of(gate, 512), cols_of(up, 512)]
    return by_columns(gate_up_kernel, (rows, gate, up), specs, 3, gate.shape[1], earlier, 2)


def down(act, weight, *earlier):
    specs = [held_rows(act), cols_of(weight, 512)]
    return by_columns(down_kernel, (act, weight), specs, 1, weight.shape[1], earlier)[0]


def act_back(grads, weight, gate, up, *earlier):
    specs = [held_rows(grads), rows_of(weight, 512), tiles_of(gate, 512), tiles_of(up, 512)]
    return by_columns(act_back_kernel, (grads, weight, gate, up), specs, 2, gate.shape[1], earlier)


def hidden_back(dgate, gate, dup, up, *earlier):
    specs = [held_rows(dgate), rows_of(gate, 512), held_rows(dup), rows_of(up, 512)]
    return by_columns(hidden_back_kernel, (dgate, gate, dup, up), specs, 1, gate.shape[0], earlier, 2)[0]


def weight_grad(former, latter, *earlier):
    rows, cols = former.shape[1], latter.shape[1]
    block = min(512, rows)
    specs = [
        pl.BlockSpec((former.shape[0], block), lambda j: (0, j)),
        pl.BlockSpec(latter.shape, lambda j: (0, 0)),
    ]
    return pl.pallas_call(
        ordered(weight_kernel, 2, earlier),
        grid=(rows // block,),
        in_specs=specs + [UNREAD] * len(earlier),
        out_specs=pl.BlockSpec((block, cols), lambda j: (j, 0)),
        out_shape=jax.ShapeDtypeStruct((rows, cols), BF16),
        compiler_params=pltpu.CompilerParams(vmem_limit_bytes=56 << 20),
        cost_estimate=cost(former.shape[0] * rows * cols * 2),
    )(former, latter, *earlier)


def project_kernel(rows_ref, weight_ref, out_ref, squares_ref):
    width = weight_ref.shape[1] // 3
    proj = dot_nn(rows_ref[...], weight_ref[...])
    out_ref[...] = proj
    squares = (proj[:, : 2 * width] * proj[:, : 2 * width]).astype(BF16)
    part = lax.broadcasted_iota(jnp.int32, (8, 2 * width), 1) // width
    chosen = part == lax.broadcasted_iota(jnp.int32, (8, 2 * width), 0)
    squares_ref[...] = dot_nt(chosen.astype(BF16), squares)


def project(rows, weight):
    count, depth = rows.shape
    block = min(512, count)
    cols = weight.shape[1]
    return pl.pallas_call(
        project_kernel,
        grid=(count // block,),
        in_specs=[
            pl.BlockSpec((block, depth), lambda i: (i, 0)),
            pl.BlockSpec(weight.shape, lambda i: (0, 0)),
        ],
        out_specs=[
            pl.BlockSpec((block, cols), lambda i: (i, 0)),
            pl.BlockSpec((8, block), lambda i: (0, i)),
        ],
        out_shape=[
            jax.ShapeDtypeStruct((count, cols), F32),
            jax.ShapeDtypeStruct((8, count), F32),
        ],
        compiler_params=pltpu.CompilerParams(vmem_limit_bytes=48 << 20),
        cost_estimate=cost(count * depth * cols * 2),
    )(rows, weight)


def prepare_kernel(proj_ref, scale_ref, gain_ref, cos_ref, sin_ref, q_ref, k_ref, v_ref):
    width = q_ref.shape[1]
    cosine, sine = cos_ref[...], sin_ref[...]
    for part, out_ref in ((0, q_ref), (1, k_ref)):
        scale = scale_ref[:, part : part + 1]
        for low in range(0, width, HEAD_DIM):
            cols = slice(part * width + low, part * width + low + HEAD_DIM)
            normed = proj_ref[:, cols] * scale * gain_ref[:, cols]
            turned = normed * cosine + pltpu.roll(normed, HEAD_DIM // 2, 1) * sine
            out_ref[:, low : low + HEAD_DIM] = turned.astype(BF16)
    v_ref[...] = proj_ref[:, 2 * width :].astype(BF16)


def prepare(proj, scales, gains, cosine, sine):
    rows, width3 = proj.shape
    width = width3 // 3
    block = min(512, rows)
    by_rows = lambda cols: pl.BlockSpec((block, cols), lambda i: (i, 0))
    return pl.pallas_call(
        prepare_kernel,
        grid=(rows // block,),
        in_specs=[
            by_rows(width3),
            by_rows(2),
            pl.BlockSpec((1, 2 * width), lambda i: (0, 0)),
            by_rows(HEAD_DIM),
            by_rows(HEAD_DIM),
        ],
        out_specs=[by_rows(width)] * 3,
        out_shape=[jax.ShapeDtypeStruct((rows, width), BF16)] * 3,
        cost_estimate=cost(rows * width3 * 3600),
    )(proj, scales, gains, cosine, sine)


def unprepare_kernel(
    dq_ref, dk_ref, dv_ref, proj_ref, scale_ref, inner_ref, gain_ref, cos_ref, sin_ref, out_ref, sum_ref
):
    width = dq_ref.shape[1]

    @pl.when(pl.program_id(0) == 0)
    def _():
        sum_ref[...] = jnp.zeros_like(sum_ref)

    cosine, sine = cos_ref[...], sin_ref[...]
    for part, in_ref in ((0, dq_ref), (1, dk_ref)):
        scale = scale_ref[:, part : part + 1]
        inner = inner_ref[:, part : part + 1]
        for low in range(0, width, HEAD_DIM):
            cols = slice(part * width + low, part * width + low + HEAD_DIM)
            turned = in_ref[:, low : low + HEAD_DIM].astype(F32)
            normed = turned * cosine - pltpu.roll(turned, HEAD_DIM // 2, 1) * sine
            scaled = proj_ref[:, cols] * scale
            sum_ref[:, cols] += jnp.sum(normed * scaled, axis=0, keepdims=True)
            result = scale * (normed * gain_ref[:, cols] - scaled * inner)
            out_ref[:, cols] = result.astype(BF16)
    out_ref[:, 2 * width :] = dv_ref[...]


def unprepare(dq, dk, dv, proj, scales, inner, gains, cosine, sine):
    rows, width3 = proj.shape
    width = width3 // 3
    block = min(512, rows)
    by_rows = lambda cols: pl.BlockSpec((block, cols), lambda i: (i, 0))
    fixed = pl.BlockSpec((1, 2 * width), lambda i: (0, 0))
    return pl.pallas_call(
        unprepare_kernel,
        grid=(rows // block,),
        in_specs=[by_rows(width)] * 3
        + [by_rows(width3), by_rows(2), by_rows(2), fixed, by_rows(HEAD_DIM), by_rows(HEAD_DIM)],
        out_specs=[by_rows(width3), fixed],
        out_shape=[
            jax.ShapeDtypeStruct((rows, width3), BF16),
            jax.ShapeDtypeStruct((1, 2 * width), F32),
        ],
        cost_estimate=cost(rows * width3 * 4700),
    )(dq, dk, dv, proj, scales, inner, gains, cosine, sine)


def visible_mask(first, keys, rows, starts):
    key_ids = lax.broadcasted_iota(jnp.int32, (keys, rows), 0)
    query_ids = first + lax.broadcasted_iota(jnp.int32, (keys, rows), 1)
    return (key_ids <= query_ids) & (key_ids >= starts)


def forward_kernel(q_ref, k_ref, v_ref, start_ref, o_ref, lse_ref, *, factor, blocks):
    block = lse_ref.shape[-1]
    whole = blocks * block
    for turn in range(blocks):

        @pl.when(pl.program_id(2) == turn)
        def _():
            keys = (turn + 1) * block
            queries = q_ref[...].reshape(block, HEAD_DIM)
            keys_all = k_ref[...].reshape(whole, HEAD_DIM)[:keys]
            values = v_ref[...].reshape(whole, HEAD_DIM)[:keys]
            scores = dot_nt(keys_all, queries) * factor
            visible = visible_mask(turn * block, keys, block, start_ref[0])
            scores = jnp.where(visible, scores, -1e30)
            top = jnp.max(scores, axis=0, keepdims=True)
            expo = jnp.exp(scores - top)
            total = jnp.sum(expo, axis=0, keepdims=True)
            outcome = dot_tn(values, expo.astype(BF16)) / total
            o_ref[...] = outcome.T.astype(BF16).reshape(o_ref.shape)
            lse_ref[0, 0] = top + jnp.log(total)


def backward_kernel(
    q_ref, k_ref, v_ref, start_ref, do_ref, lse_ref, dq_ref, dk_ref, dv_ref, dk_sum, dv_sum, *, factor, blocks
):
    block = lse_ref.shape[-1]
    whole = blocks * block

    @pl.when(pl.program_id(2) == 0)
    def _():
        dk_sum[...] = jnp.zeros_like(dk_sum)
        dv_sum[...] = jnp.zeros_like(dv_sum)

    for turn in range(blocks):

        @pl.when(pl.program_id(2) == turn)
        def _():
            keys = (turn + 1) * block
            queries = q_ref[...].reshape(block, HEAD_DIM)
            grads = do_ref[...].reshape(block, HEAD_DIM)
            keys_all = k_ref[...].reshape(whole, HEAD_DIM)[:keys]
            values = v_ref[...].reshape(whole, HEAD_DIM)[:keys]
            scores = dot_nt(keys_all, queries) * factor
            visible = visible_mask(turn * block, keys, block, start_ref[0])
            soft = jnp.where(visible, jnp.exp(scores - lse_ref[0, 0]), 0.0)
            dv_sum[:keys] += dot_nn(soft.astype(BF16), grads)
            dsoft = dot_nt(values, grads)
            delta = jnp.sum(dsoft * soft, axis=0, keepdims=True)
            dscores = (soft * (dsoft - delta)).astype(BF16)
            dk_sum[:keys] += dot_nn(dscores, queries)
            dq = dot_tn(keys_all, dscores) * factor
            dq_ref[...] = dq.T.astype(BF16).reshape(dq_ref.shape)

    @pl.when(pl.program_id(2) == blocks - 1)
    def _():
        dk_ref[...] = (dk_sum[...] * factor).astype(BF16).reshape(dk_ref.shape)
        dv_ref[...] = dv_sum[...].astype(BF16).reshape(dv_ref.shape)


def attention_specs(shape):
    groups, count, rows, width = shape
    whole = groups * rows
    block = min(512, whole)
    per = block // rows
    some = pl.BlockSpec((per, 1, rows, HEAD_DIM), lambda b, h, i: (i, b, 0, h))
    every = pl.BlockSpec((groups, 1, rows, HEAD_DIM), lambda b, h, i: (0, b, 0, h))
    starts = pl.BlockSpec((1, 1, block), lambda b, h, i: (b, 0, i))
    sums = pl.BlockSpec((1, 1, 1, block), lambda b, h, i: (b, h, 0, i))
    heads = width // HEAD_DIM
    pairs = count * heads * whole * whole
    return some, every, starts, sums, (count, heads, whole // block), whole, pairs


def attend_forward(queries, keys, values, starts, factor, *earlier):
    some, every, start_spec, sums, grid, whole, pairs = attention_specs(queries.shape)
    return pl.pallas_call(
        ordered(functools.partial(forward_kernel, factor=factor, blocks=grid[2]), 4, earlier),
        grid=grid,
        in_specs=[some, every, every, start_spec] + [UNREAD] * len(earlier),
        out_specs=[some, sums],
        out_shape=[
            jax.ShapeDtypeStruct(queries.shape, BF16),
            jax.ShapeDtypeStruct((grid[0], grid[1], 1, whole), F32),
        ],
        compiler_params=pltpu.CompilerParams(vmem_limit_bytes=48 << 20),
        cost_estimate=cost(pairs * HEAD_DIM * 11),
    )(queries, keys, values, starts, *earlier)


def attend_backward(queries, keys, values, starts, grads, log_sums, factor, *earlier):
    some, every, start_spec, sums, grid, whole, pairs = attention_specs(queries.shape)
    return pl.pallas_call(
        ordered(functools.partial(backward_kernel, factor=factor, blocks=grid[2]), 6, earlier),
        grid=grid,
        in_specs=[some, every, every, start_spec, some, sums] + [UNREAD] * len(earlier),
        out_specs=[some, every, every],
        out_shape=[jax.ShapeDtypeStruct(queries.shape, BF16)] * 3,
        scratch_shapes=[pltpu.VMEM((whole, HEAD_DIM), F32)] * 2,
        compiler_params=pltpu.CompilerParams(vmem_limit_bytes=52 << 20),
        cost_estimate=cost(pairs * HEAD_DIM * 20),
    )(queries, keys, values, starts, grads, log_sums, *earlier)


def on_device(
    tokens,
    positions,
    out_grad,
    w_query,
    w_key,
    w_value,
    w_output,
    query_gain,
    key_gain,
    attn_gain,
    w_gate,
    w_up,
    w_down,
    mlp_gain,
):
    fsdp, seq = lax.axis_size("fsdp"), lax.axis_size("seq")
    row, place = lax.axis_index("fsdp"), lax.axis_index("seq")
    groups = seq // GROUP
    factor = HEAD_DIM ** (-0.5)
    count = tokens.shape[0] * tokens.shape[1]
    tok_count, width = tokens.shape[2], tokens.shape[3]
    own_rows = count * tok_count
    local_width = width // seq
    hidden_width = w_gate.shape[1] // GROUP
    share = w_query.shape[0]
    down_share = w_down.shape[0]
    head_shape = (seq, count, tok_count, local_width)

    inputs = tokens.reshape(own_rows, width)
    grad_rows = out_grad.reshape(own_rows, width).astype(F32)
    inputs_all = lax.all_gather(inputs, "seq", axis=0, tiled=True)

    qkv_weight = lax.all_to_all(
        jnp.stack([w_query, w_key, w_value]), "seq", split_axis=2, concat_axis=1, tiled=True
    )
    qkv_weight = jnp.moveaxis(qkv_weight, 0, 1).reshape(seq * share, 3 * local_width)
    qkv_weight = gather_placed(qkv_weight, "fsdp")

    own_gains = jnp.stack([query_gain, key_gain, attn_gain, mlp_gain]).astype(F32)
    small = jnp.concatenate([own_gains.reshape(-1), positions.reshape(-1).astype(F32)])
    small = lax.dynamic_update_index_in_dim(jnp.zeros((seq, small.shape[0]), F32), small, place, 0)
    small = sum_small(small, "seq")
    gains = small[:, : 4 * share].reshape(seq, 4, share)
    gains = lax.dynamic_update_index_in_dim(jnp.zeros((fsdp, seq, 4, share), F32), gains, row, 0)
    gains = jnp.moveaxis(sum_small(gains, "fsdp"), 2, 0).reshape(4, 1, width)
    a_gain, m_gain = gains[2], gains[3]
    qk_gain = lax.dynamic_slice_in_dim(gains[:2], place * local_width, local_width, 2)
    qk_gain = qk_gain.reshape(1, 2 * local_width)
    places = small[:, 4 * share :].reshape(seq, count, tok_count)
    cosine, sine = rope_tables(places.reshape(-1))
    order = jnp.arange(seq * tok_count, dtype=jnp.int32).reshape(seq, 1, tok_count)
    starts = jnp.moveaxis(order - places.astype(jnp.int32), 0, 1).reshape(count, 1, seq * tok_count)

    def columns(weight):
        part = weight.reshape(share, fsdp * groups, GROUP, down_share)
        part = jnp.moveaxis(part, 2, 0).reshape(1, GROUP, share, hidden_width)
        part = jnp.broadcast_to(part, (groups, GROUP, share, hidden_width))
        part = part.reshape(seq * share, hidden_width)
        return lax.all_to_all(part, "seq", split_axis=0, concat_axis=0, tiled=True)

    inputs_all = after(inputs_all, qkv_weight, cosine, sine, starts, gains)
    g_part = columns(after(w_gate, inputs_all))
    o_weight = lax.all_gather(w_output, BOTH, axis=0, tiled=True)
    proj, squares = project(inputs_all, qkv_weight)
    scales = lax.rsqrt(sum_small(squares[:2], "seq") / width + EPSILON).T
    rotated = prepare(proj, scales, qk_gain, cosine, sine)
    g_part = after(g_part, *rotated)
    u_part = columns(after(w_up, g_part))
    g_weight = lax.all_gather(g_part, "fsdp", axis=0, tiled=True)
    rotated = [v.reshape(head_shape) for v in rotated]
    attended, log_sums = attend_forward(*rotated, starts, factor)
    attended = after(attended, u_part)
    attn_rows = lax.all_to_all(
        attended.reshape(seq, own_rows, local_width), "seq", split_axis=0, concat_axis=0, tiled=True
    )
    attn_rows = jnp.moveaxis(attn_rows, 0, 1).reshape(own_rows, width)

    a_proj = dot_nn(attn_rows, o_weight)
    a_scale = inv_rms(a_proj)
    hidden = inputs.astype(F32) + a_proj * a_scale * a_gain
    d_part = gather_outer(after(w_down, u_part))
    u_weight, d_weight = (lax.all_gather(v, "fsdp", axis=0, tiled=True) for v in (u_part, d_part))
    hidden_low = gather_group(hidden.astype(BF16))
    gate, up, act = gate_up(hidden_low, g_weight, u_weight)
    m_proj = scatter_far(scatter_near(down(act, d_weight)))
    m_scale = inv_rms(m_proj)
    mixed = (hidden + m_proj * m_scale * m_gain).astype(BF16)

    grad_mproj, grad_mgain = norm_back(grad_rows, m_proj, m_scale, m_gain)
    grad_mproj = gather_group(grad_mproj.astype(BF16))

    def over_rows(part):
        return lax.psum_scatter(part, "fsdp", scatter_dimension=0, tiled=True)

    def columns_sent(part):
        return lax.all_to_all(part, "seq", split_axis=0, concat_axis=0, tiled=True)

    def columns_joined(part):
        part = part.reshape(groups, GROUP, share, fsdp * groups, down_share)
        return jnp.moveaxis(part.astype(F32).sum(axis=0), 0, 2).reshape(share, -1)

    dgate, dup = act_back(grad_mproj, d_weight, gate, up)
    down_grad = weight_grad(act, grad_mproj, dgate)
    share_down = over_rows(down_grad)
    grads = hidden_back(dgate, g_weight, dup, u_weight, down_grad)
    grads = scatter_near(grads)
    gate_grad = weight_grad(hidden_low, dgate, grads)
    share_gate = over_rows(gate_grad)
    grad_hidden = grad_rows + scatter_far(grads, gate_grad)

    grad_aproj, grad_again = norm_back(grad_hidden, a_proj, a_scale, a_gain)
    grad_aproj = after(grad_aproj.astype(BF16), share_down)
    grad_attn = dot_nt(grad_aproj, o_weight).astype(BF16)
    grad_attn = jnp.moveaxis(grad_attn.reshape(own_rows, seq, local_width), 1, 0)
    grad_heads = lax.all_to_all(grad_attn, "seq", split_axis=0, concat_axis=0, tiled=True)
    up_grad = weight_grad(hidden_low, dup, gate_grad, grad_attn)
    share_up = over_rows(up_grad)
    o_grad = weight_grad(attn_rows, grad_aproj, up_grad)
    share_output = over_rows(o_grad)
    grad_heads = after(grad_heads, o_grad, share_gate)
    share_down = scatter_outer(after(share_down, grad_heads))
    dq, dk, dv = attend_backward(
        *rotated, starts, grad_heads.reshape(head_shape), log_sums, factor
    )
    dq = after(dq, share_down)
    share_gate = columns_sent(after(share_gate, dq))
    dq, dk, dv = (v.reshape(seq * own_rows, local_width) for v in (dq, dk, dv))
    q_rot, k_rot = (v.reshape(seq * own_rows, local_width) for v in rotated[:2])
    inner = jnp.stack(
        [
            jnp.sum(dq.astype(F32) * q_rot.astype(F32), axis=1),
            jnp.sum(dk.astype(F32) * k_rot.astype(F32), axis=1),
        ]
    )
    inner = sum_small(inner, "seq") / width
    grad_qkv, gain_sums = unprepare(
        dq, dk, after(dv, share_up), proj, scales, inner.T, qk_gain, cosine, sine
    )
    partial = dot_nt(grad_qkv, qkv_weight).astype(BF16)
    partial = after(partial, share_gate)
    qkv_grad = weight_grad(inputs_all, grad_qkv, partial)
    qkv_grad = after(qkv_grad, share_output)
    share_output = lax.all_to_all(share_output, "seq", split_axis=0, concat_axis=0, tiled=True)
    middle = (share_output,)
    share_output = share_output.astype(F32).reshape(seq, share, width).sum(axis=0)
    share_gate = columns_joined(share_gate)
    share_up = columns_sent(after(share_up, partial))
    early = (share_up,)
    share_up = columns_joined(share_up)
    share_qkv = over_rows(qkv_grad)
    share_qkv = lax.all_to_all(
        share_qkv.reshape(seq, share, 3 * local_width), "seq", split_axis=0, concat_axis=0, tiled=True
    )
    share_qkv = share_qkv.reshape(seq, share, 3, local_width).transpose(2, 1, 0, 3)
    share_qkv = share_qkv.reshape(3, share, width).astype(F32)
    slots = lax.dynamic_update_slice_in_dim(
        jnp.zeros((2, width), F32), gain_sums.reshape(2, local_width), place * local_width, 1
    )
    slots = jnp.concatenate([slots, grad_again[None], grad_mgain[None]])
    slots = sum_small(sum_small(slots, "fsdp"), "seq")
    gain_grads = lax.dynamic_slice_in_dim(slots, (row * seq + place) * share, share, 1)
    late = (share_gate, share_up, share_output, share_qkv, gain_grads)
    grad_inputs = scatter_line(partial, {1: early, 2: middle, seq // 2 - 1: late})
    input_grad = (grad_hidden + grad_inputs).astype(BF16)
    return (
        mixed.reshape(tokens.shape),
        input_grad.reshape(tokens.shape),
        share_qkv[0],
        share_qkv[1],
        share_qkv[2],
        share_output,
        gain_grads[0],
        gain_grads[1],
        gain_grads[2],
        share_gate,
        share_up,
        share_down,
        gain_grads[3],
    )


def solution(mesh):
    rows = P(BOTH, None)
    flat = P(BOTH)
    acts = P(None, "fsdp", "seq", None)
    return jax.shard_map(
        on_device,
        mesh=mesh,
        in_specs=(acts, P(None, "fsdp", "seq"), acts, rows, rows, rows, rows, flat, flat, flat)
        + (rows, rows, rows, flat),
        out_specs=(acts, acts, rows, rows, rows, rows, flat, flat, flat, rows, rows, rows, flat),
        check_vma=False,
    )
```

```python
import functools

import jax
import jax.numpy as jnp
from jax import lax
from jax.experimental import pallas as pl
from jax.experimental.pallas import tpu as pltpu
from jax.sharding import PartitionSpec as P

HEADS = 16
HEAD_DIM = 128

EPSILON = 1e-06
THETA = 500000.0

BF16 = jnp.bfloat16
F32 = jnp.float32
BOTH = ("fsdp", "seq")

GROUP = 4

UNREAD = pl.BlockSpec(memory_space=pl.ANY)
NO_COST = pl.CostEstimate(flops=0, bytes_accessed=0, transcendentals=0)


def cost(flops):
    return pl.CostEstimate(flops=int(flops * 1), bytes_accessed=0, transcendentals=0)


def dot_nn(former, latter):
    return jnp.dot(former, latter, preferred_element_type=F32)


def dot_tn(former, latter):
    return lax.dot_general(former, latter, (((0,), (0,)), ((), ())), preferred_element_type=F32)


def dot_nt(former, latter):
    return lax.dot_general(former, latter, (((1,), (1,)), ((), ())), preferred_element_type=F32)


def inv_rms(values):
    return lax.rsqrt(jnp.mean(values * values, axis=-1, keepdims=True) + EPSILON)


def norm_back(incoming, values, factor, gain_row):
    weighted = incoming * gain_row
    inner_mean = jnp.mean(weighted * values, axis=-1, keepdims=True)
    result_grad = factor * (weighted - values * factor * factor * inner_mean)
    return (result_grad, jnp.sum(incoming * values * factor, axis=0))


def rope_tables(places_pos):
    half = HEAD_DIM // 2
    exponent = jnp.arange(0, half, dtype=F32) * (2.0 / HEAD_DIM)
    frequency = THETA ** (-exponent)
    angles = places_pos.astype(F32)[:, None] * frequency[None, :]
    cosine, sine = jnp.cos(angles), jnp.sin(angles)
    return (
        jnp.concatenate([cosine, cosine], axis=-1),
        jnp.concatenate([-sine, sine], axis=-1),
    )


def bits_of(size):
    return [1 << i for i in range(size.bit_length() - 1)]


def exchange(values, axis, bit):
    return lax.ppermute(values, axis, [(i, i ^ bit) for i in range(lax.axis_size(axis))])


def sum_small(values, axis):
    for bit in bits_of(lax.axis_size(axis)):
        values = values + exchange(values, axis, bit)
    return values


def after(values, *earlier):
    return pl.pallas_call(
        lambda *refs: None,
        in_specs=[UNREAD] * (1 + len(earlier)),
        out_specs=UNREAD,
        out_shape=jax.ShapeDtypeStruct(values.shape, values.dtype),
        input_output_aliases={0: 0},
        cost_estimate=NO_COST,
    )(values, *earlier)


def gather_group(values):
    near, far = 1, 2
    other = exchange(values, "seq", far)
    return jnp.concatenate(
        [values, other, exchange(values, "seq", near), exchange(other, "seq", near)]
    )


def halve(held, bits, axis, stride=1):
    for i, bit in enumerate(bits):
        sent = {m: exchange(v, axis, bit * stride) for m, v in held.items() if m & bit}
        held = {m: held[m].astype(F32) + sent[m ^ bit].astype(F32) for m in held if not m & bit}
        if i < len(bits) - 1:
            held = {m: v.astype(BF16) for m, v in held.items()}
    return held[0]


def scatter_near(values):
    rows = values.shape[0] // 2
    return values[:rows].astype(F32) + exchange(values[rows:], "seq", 1).astype(F32)


def scatter_far(half, *earlier):
    rows = half.shape[0] // 2
    return half[:rows] + after(exchange(half[rows:].astype(BF16), "seq", 2), *earlier).astype(F32)


def gather_outer(values):
    groups = lax.axis_size("seq") // GROUP
    own = lax.axis_index("seq") // GROUP
    found = {0: values}
    for bit in bits_of(groups):
        found |= {m ^ bit: exchange(v, "seq", bit * GROUP) for m, v in found.items()}
    blocks = []
    for i in range(groups):
        block = found[0]
        for m in range(1, groups):
            block = jnp.where((own ^ i) == m, found[m], block)
        blocks.append(block)
    return jnp.concatenate(blocks)


def scatter_outer(values):
    groups = lax.axis_size("seq") // GROUP
    own = lax.axis_index("seq") // GROUP
    rows = values.shape[0] // groups
    held = {
        m: lax.dynamic_slice_in_dim(values, (own ^ m) * rows, rows, 0) for m in range(groups)
    }
    return halve(held, bits_of(groups)[::-1], "seq", GROUP)


def shift(values, step):
    size = lax.axis_size("seq")
    pairs = [(i, i + 2 * step) for i in range(size) if 0 <= i + 2 * step < size]
    return lax.ppermute(values, "seq", pairs)


def gather_placed(values, axis):
    size, own = lax.axis_size(axis), lax.axis_index(axis)
    bits, rows = bits_of(size), values.shape[0]
    parts = [(0, values, bits[::-1])]
    if axis == "fsdp":
        half = rows // 2
        parts = [(0, values[:half], bits), (half, values[half:], bits[::-1])]
    out = jnp.zeros((size * rows, values.shape[1]), values.dtype)
    for first, part, order in parts:
        found = {0: part}
        for bit in order:
            found |= {m ^ bit: exchange(v, axis, bit) for m, v in found.items()}
        for m, v in found.items():
            out = lax.dynamic_update_slice_in_dim(out, v, (own ^ m) * rows + first, 0)
    return out


def scatter_line(values, earlier):
    size, place = lax.axis_size("seq"), lax.axis_index("seq")
    pairs, pair, core = size // 2, place // 2, place % 2
    rows = values.shape[0] // size
    blocks = values.reshape(pairs, 2, rows, values.shape[1])
    sent = exchange(lax.dynamic_index_in_dim(blocks, 1 - core, 1, keepdims=False), "seq", 1)
    kept = lax.dynamic_index_in_dim(blocks, core, 1, keepdims=False)
    blocks = (kept.astype(F32) + sent.astype(F32)).astype(BF16)

    def block_at(place):
        place = jnp.clip(place, 0, pairs - 1)
        return lax.dynamic_index_in_dim(blocks, place, 0, keepdims=False)

    up = down = None
    for far in range(pairs - 1, 0, -1):
        next_up, next_down = block_at(pair + far), block_at(pair - far)
        if up is not None:
            next_up = (next_up.astype(F32) + up.astype(F32)).astype(BF16)
            next_down = (next_down.astype(F32) + down.astype(F32)).astype(BF16)
        up, down = shift(next_up, 1), shift(next_down, -1)
        up = after(up, down, *earlier.get(pairs - far, ()))
    return block_at(pair).astype(F32) + up.astype(F32) + down.astype(F32)


def ordered(kernel, count, earlier):
    return lambda *refs: kernel(*refs[:count], *refs[count + len(earlier) :])


def gate_up_kernel(rows_ref, gate_ref, up_ref, gate_out, up_out, act_out):
    gate = dot_nn(rows_ref[...], gate_ref[...])
    up = dot_nn(rows_ref[...], up_ref[...])
    gate_out[...] = gate.astype(BF16)
    up_out[...] = up.astype(BF16)
    act_out[...] = (gate * jax.nn.sigmoid(gate) * up).astype(BF16)


def down_kernel(act_ref, down_ref, out_ref):
    out_ref[...] = dot_nn(act_ref[...], down_ref[...]).astype(BF16)


def act_back_kernel(grad_ref, down_ref, gate_ref, up_ref, dgate_ref, dup_ref):
    dact = dot_nt(grad_ref[...], down_ref[...])
    gate, up = gate_ref[...].astype(F32), up_ref[...].astype(F32)
    sigmoid = jax.nn.sigmoid(gate)
    dgate_ref[...] = (dact * up * sigmoid * (1.0 + gate * (1.0 - sigmoid))).astype(BF16)
    dup_ref[...] = (dact * gate * sigmoid).astype(BF16)


def hidden_back_kernel(dgate_ref, gate_ref, dup_ref, up_ref, out_ref):
    total = dot_nt(dgate_ref[...], gate_ref[...]) + dot_nt(dup_ref[...], up_ref[...])
    out_ref[...] = total.astype(BF16)


def weight_kernel(former_ref, latter_ref, out_ref):
    out_ref[...] = dot_tn(former_ref[...], latter_ref[...]).astype(BF16)


def held_rows(values):
    return pl.BlockSpec((min(1024, values.shape[0]), values.shape[1]), lambda j, i: (i, 0))


def cols_of(values, block):
    return pl.BlockSpec((values.shape[0], block), lambda j, i: (0, j))


def rows_of(values, block):
    return pl.BlockSpec((block, values.shape[1]), lambda j, i: (j, 0))


def tiles_of(values, block):
    return pl.BlockSpec((min(1024, values.shape[0]), block), lambda j, i: (i, j))


def by_columns(kernel, operands, specs, outs, cols, earlier, products=1):
    rows = operands[0].shape[0]
    high = min(1024, rows)
    return pl.pallas_call(
        ordered(kernel, len(operands), earlier),
        grid=(cols // 512, rows // high),
        in_specs=specs + [UNREAD] * len(earlier),
        out_specs=[pl.BlockSpec((high, 512), lambda j, i: (i, j))] * outs,
        out_shape=[jax.ShapeDtypeStruct((rows, cols), BF16)] * outs,
        compiler_params=pltpu.CompilerParams(vmem_limit_bytes=56 << 20),
        cost_estimate=cost(products * rows * cols * operands[0].shape[1] * 2),
    )(*operands, *earlier)


def gate_up(rows, gate, up, *earlier):
    specs = [held_rows(rows), cols_of(gate, 512), cols_of(up, 512)]
    return by_columns(gate_up_kernel, (rows, gate, up), specs, 3, gate.shape[1], earlier, 2)


def down(act, weight, *earlier):
    specs = [held_rows(act), cols_of(weight, 512)]
    return by_columns(down_kernel, (act, weight), specs, 1, weight.shape[1], earlier)[0]


def act_back(grads, weight, gate, up, *earlier):
    specs = [held_rows(grads), rows_of(weight, 512), tiles_of(gate, 512), tiles_of(up, 512)]
    return by_columns(act_back_kernel, (grads, weight, gate, up), specs, 2, gate.shape[1], earlier)


def hidden_back(dgate, gate, dup, up, *earlier):
    specs = [held_rows(dgate), rows_of(gate, 512), held_rows(dup), rows_of(up, 512)]
    return by_columns(hidden_back_kernel, (dgate, gate, dup, up), specs, 1, gate.shape[0], earlier, 2)[0]


def weight_grad(former, latter, *earlier):
    rows, cols = former.shape[1], latter.shape[1]
    block = min(512, rows)
    specs = [
        pl.BlockSpec((former.shape[0], block), lambda j: (0, j)),
        pl.BlockSpec(latter.shape, lambda j: (0, 0)),
    ]
    return pl.pallas_call(
        ordered(weight_kernel, 2, earlier),
        grid=(rows // block,),
        in_specs=specs + [UNREAD] * len(earlier),
        out_specs=pl.BlockSpec((block, cols), lambda j: (j, 0)),
        out_shape=jax.ShapeDtypeStruct((rows, cols), BF16),
        compiler_params=pltpu.CompilerParams(vmem_limit_bytes=56 << 20),
        cost_estimate=cost(former.shape[0] * rows * cols * 2),
    )(former, latter, *earlier)


def project_kernel(rows_ref, weight_ref, out_ref, squares_ref):
    width = weight_ref.shape[1] // 3
    proj = dot_nn(rows_ref[...], weight_ref[...])
    out_ref[...] = proj
    squares = (proj[:, : 2 * width] * proj[:, : 2 * width]).astype(BF16)
    part = lax.broadcasted_iota(jnp.int32, (8, 2 * width), 1) // width
    chosen = part == lax.broadcasted_iota(jnp.int32, (8, 2 * width), 0)
    squares_ref[...] = dot_nt(chosen.astype(BF16), squares)


def project(rows, weight):
    count, depth = rows.shape
    block = min(512, count)
    cols = weight.shape[1]
    return pl.pallas_call(
        project_kernel,
        grid=(count // block,),
        in_specs=[
            pl.BlockSpec((block, depth), lambda i: (i, 0)),
            pl.BlockSpec(weight.shape, lambda i: (0, 0)),
        ],
        out_specs=[
            pl.BlockSpec((block, cols), lambda i: (i, 0)),
            pl.BlockSpec((8, block), lambda i: (0, i)),
        ],
        out_shape=[
            jax.ShapeDtypeStruct((count, cols), F32),
            jax.ShapeDtypeStruct((8, count), F32),
        ],
        compiler_params=pltpu.CompilerParams(vmem_limit_bytes=48 << 20),
        cost_estimate=cost(count * depth * cols * 2),
    )(rows, weight)


def prepare_kernel(proj_ref, scale_ref, gain_ref, cos_ref, sin_ref, q_ref, k_ref, v_ref):
    width = q_ref.shape[1]
    cosine, sine = cos_ref[...], sin_ref[...]
    for part, out_ref in ((0, q_ref), (1, k_ref)):
        scale = scale_ref[:, part : part + 1]
        for low in range(0, width, HEAD_DIM):
            cols = slice(part * width + low, part * width + low + HEAD_DIM)
            normed = proj_ref[:, cols] * scale * gain_ref[:, cols]
            turned = normed * cosine + pltpu.roll(normed, HEAD_DIM // 2, 1) * sine
            out_ref[:, low : low + HEAD_DIM] = turned.astype(BF16)
    v_ref[...] = proj_ref[:, 2 * width :].astype(BF16)


def prepare(proj, scales, gains, cosine, sine):
    rows, width3 = proj.shape
    width = width3 // 3
    block = min(512, rows)
    by_rows = lambda cols: pl.BlockSpec((block, cols), lambda i: (i, 0))
    return pl.pallas_call(
        prepare_kernel,
        grid=(rows // block,),
        in_specs=[
            by_rows(width3),
            by_rows(2),
            pl.BlockSpec((1, 2 * width), lambda i: (0, 0)),
            by_rows(HEAD_DIM),
            by_rows(HEAD_DIM),
        ],
        out_specs=[by_rows(width)] * 3,
        out_shape=[jax.ShapeDtypeStruct((rows, width), BF16)] * 3,
        cost_estimate=cost(rows * width3 * 3600),
    )(proj, scales, gains, cosine, sine)


def unprepare_kernel(
    dq_ref, dk_ref, dv_ref, proj_ref, scale_ref, inner_ref, gain_ref, cos_ref, sin_ref, out_ref, sum_ref
):
    width = dq_ref.shape[1]

    @pl.when(pl.program_id(0) == 0)
    def _():
        sum_ref[...] = jnp.zeros_like(sum_ref)

    cosine, sine = cos_ref[...], sin_ref[...]
    for part, in_ref in ((0, dq_ref), (1, dk_ref)):
        scale = scale_ref[:, part : part + 1]
        inner = inner_ref[:, part : part + 1]
        for low in range(0, width, HEAD_DIM):
            cols = slice(part * width + low, part * width + low + HEAD_DIM)
            turned = in_ref[:, low : low + HEAD_DIM].astype(F32)
            normed = turned * cosine - pltpu.roll(turned, HEAD_DIM // 2, 1) * sine
            scaled = proj_ref[:, cols] * scale
            sum_ref[:, cols] += jnp.sum(normed * scaled, axis=0, keepdims=True)
            result = scale * (normed * gain_ref[:, cols] - scaled * inner)
            out_ref[:, cols] = result.astype(BF16)
    out_ref[:, 2 * width :] = dv_ref[...]


def unprepare(dq, dk, dv, proj, scales, inner, gains, cosine, sine):
    rows, width3 = proj.shape
    width = width3 // 3
    block = min(512, rows)
    by_rows = lambda cols: pl.BlockSpec((block, cols), lambda i: (i, 0))
    fixed = pl.BlockSpec((1, 2 * width), lambda i: (0, 0))
    return pl.pallas_call(
        unprepare_kernel,
        grid=(rows // block,),
        in_specs=[by_rows(width)] * 3
        + [by_rows(width3), by_rows(2), by_rows(2), fixed, by_rows(HEAD_DIM), by_rows(HEAD_DIM)],
        out_specs=[by_rows(width3), fixed],
        out_shape=[
            jax.ShapeDtypeStruct((rows, width3), BF16),
            jax.ShapeDtypeStruct((1, 2 * width), F32),
        ],
        cost_estimate=cost(rows * width3 * 4700),
    )(dq, dk, dv, proj, scales, inner, gains, cosine, sine)


def visible_mask(first, keys, rows, starts):
    key_ids = lax.broadcasted_iota(jnp.int32, (keys, rows), 0)
    query_ids = first + lax.broadcasted_iota(jnp.int32, (keys, rows), 1)
    return (key_ids <= query_ids) & (key_ids >= starts)


def forward_kernel(q_ref, k_ref, v_ref, start_ref, o_ref, lse_ref, *, factor, blocks):
    block = lse_ref.shape[-1]
    whole = blocks * block
    for turn in range(blocks):

        @pl.when(pl.program_id(2) == turn)
        def _():
            keys = (turn + 1) * block
            queries = q_ref[...].reshape(block, HEAD_DIM)
            keys_all = k_ref[...].reshape(whole, HEAD_DIM)[:keys]
            values = v_ref[...].reshape(whole, HEAD_DIM)[:keys]
            scores = dot_nt(keys_all, queries) * factor
            visible = visible_mask(turn * block, keys, block, start_ref[0])
            scores = jnp.where(visible, scores, -1e30)
            top = jnp.max(scores, axis=0, keepdims=True)
            expo = jnp.exp(scores - top)
            total = jnp.sum(expo, axis=0, keepdims=True)
            outcome = dot_tn(values, expo.astype(BF16)) / total
            o_ref[...] = outcome.T.astype(BF16).reshape(o_ref.shape)
            lse_ref[0, 0] = top + jnp.log(total)


def backward_kernel(
    q_ref, k_ref, v_ref, start_ref, do_ref, lse_ref, dq_ref, dk_ref, dv_ref, dk_sum, dv_sum, *, factor, blocks
):
    block = lse_ref.shape[-1]
    whole = blocks * block

    @pl.when(pl.program_id(2) == 0)
    def _():
        dk_sum[...] = jnp.zeros_like(dk_sum)
        dv_sum[...] = jnp.zeros_like(dv_sum)

    for turn in range(blocks):

        @pl.when(pl.program_id(2) == turn)
        def _():
            keys = (turn + 1) * block
            queries = q_ref[...].reshape(block, HEAD_DIM)
            grads = do_ref[...].reshape(block, HEAD_DIM)
            keys_all = k_ref[...].reshape(whole, HEAD_DIM)[:keys]
            values = v_ref[...].reshape(whole, HEAD_DIM)[:keys]
            scores = dot_nt(keys_all, queries) * factor
            visible = visible_mask(turn * block, keys, block, start_ref[0])
            soft = jnp.where(visible, jnp.exp(scores - lse_ref[0, 0]), 0.0)
            dv_sum[:keys] += dot_nn(soft.astype(BF16), grads)
            dsoft = dot_nt(values, grads)
            delta = jnp.sum(dsoft * soft, axis=0, keepdims=True)
            dscores = (soft * (dsoft - delta)).astype(BF16)
            dk_sum[:keys] += dot_nn(dscores, queries)
            dq = dot_tn(keys_all, dscores) * factor
            dq_ref[...] = dq.T.astype(BF16).reshape(dq_ref.shape)

    @pl.when(pl.program_id(2) == blocks - 1)
    def _():
        dk_ref[...] = (dk_sum[...] * factor).astype(BF16).reshape(dk_ref.shape)
        dv_ref[...] = dv_sum[...].astype(BF16).reshape(dv_ref.shape)


def attention_specs(shape):
    groups, count, rows, width = shape
    whole = groups * rows
    block = min(512, whole)
    per = block // rows
    some = pl.BlockSpec((per, 1, rows, HEAD_DIM), lambda b, h, i: (i, b, 0, h))
    every = pl.BlockSpec((groups, 1, rows, HEAD_DIM), lambda b, h, i: (0, b, 0, h))
    starts = pl.BlockSpec((1, 1, block), lambda b, h, i: (b, 0, i))
    sums = pl.BlockSpec((1, 1, 1, block), lambda b, h, i: (b, h, 0, i))
    heads = width // HEAD_DIM
    pairs = count * heads * whole * whole
    return some, every, starts, sums, (count, heads, whole // block), whole, pairs


def attend_forward(queries, keys, values, starts, factor, *earlier):
    some, every, start_spec, sums, grid, whole, pairs = attention_specs(queries.shape)
    return pl.pallas_call(
        ordered(functools.partial(forward_kernel, factor=factor, blocks=grid[2]), 4, earlier),
        grid=grid,
        in_specs=[some, every, every, start_spec] + [UNREAD] * len(earlier),
        out_specs=[some, sums],
        out_shape=[
            jax.ShapeDtypeStruct(queries.shape, BF16),
            jax.ShapeDtypeStruct((grid[0], grid[1], 1, whole), F32),
        ],
        compiler_params=pltpu.CompilerParams(vmem_limit_bytes=48 << 20),
        cost_estimate=cost(pairs * HEAD_DIM * 11),
    )(queries, keys, values, starts, *earlier)


def attend_backward(queries, keys, values, starts, grads, log_sums, factor, *earlier):
    some, every, start_spec, sums, grid, whole, pairs = attention_specs(queries.shape)
    return pl.pallas_call(
        ordered(functools.partial(backward_kernel, factor=factor, blocks=grid[2]), 6, earlier),
        grid=grid,
        in_specs=[some, every, every, start_spec, some, sums] + [UNREAD] * len(earlier),
        out_specs=[some, every, every],
        out_shape=[jax.ShapeDtypeStruct(queries.shape, BF16)] * 3,
        scratch_shapes=[pltpu.VMEM((whole, HEAD_DIM), F32)] * 2,
        compiler_params=pltpu.CompilerParams(vmem_limit_bytes=52 << 20),
        cost_estimate=cost(pairs * HEAD_DIM * 20),
    )(queries, keys, values, starts, grads, log_sums, *earlier)


def on_device(
    tokens,
    positions,
    out_grad,
    w_query,
    w_key,
    w_value,
    w_output,
    query_gain,
    key_gain,
    attn_gain,
    w_gate,
    w_up,
    w_down,
    mlp_gain,
):
    fsdp, seq = lax.axis_size("fsdp"), lax.axis_size("seq")
    row, place = lax.axis_index("fsdp"), lax.axis_index("seq")
    groups = seq // GROUP
    factor = HEAD_DIM ** (-0.5)
    count = tokens.shape[0] * tokens.shape[1]
    tok_count, width = tokens.shape[2], tokens.shape[3]
    own_rows = count * tok_count
    local_width = width // seq
    hidden_width = w_gate.shape[1] // GROUP
    share = w_query.shape[0]
    down_share = w_down.shape[0]
    head_shape = (seq, count, tok_count, local_width)

    inputs = tokens.reshape(own_rows, width)
    grad_rows = out_grad.reshape(own_rows, width).astype(F32)
    inputs_all = lax.all_gather(inputs, "seq", axis=0, tiled=True)

    qkv_weight = lax.all_to_all(
        jnp.stack([w_query, w_key, w_value]), "seq", split_axis=2, concat_axis=1, tiled=True
    )
    qkv_weight = jnp.moveaxis(qkv_weight, 0, 1).reshape(seq * share, 3 * local_width)
    qkv_weight = gather_placed(qkv_weight, "fsdp")

    own_gains = jnp.stack([query_gain, key_gain, attn_gain, mlp_gain]).astype(F32)
    small = jnp.concatenate([own_gains.reshape(-1), positions.reshape(-1).astype(F32)])
    small = lax.dynamic_update_index_in_dim(jnp.zeros((seq, small.shape[0]), F32), small, place, 0)
    small = sum_small(small, "seq")
    gains = small[:, : 4 * share].reshape(seq, 4, share)
    gains = lax.dynamic_update_index_in_dim(jnp.zeros((fsdp, seq, 4, share), F32), gains, row, 0)
    gains = jnp.moveaxis(sum_small(gains, "fsdp"), 2, 0).reshape(4, 1, width)
    a_gain, m_gain = gains[2], gains[3]
    qk_gain = lax.dynamic_slice_in_dim(gains[:2], place * local_width, local_width, 2)
    qk_gain = qk_gain.reshape(1, 2 * local_width)
    places = small[:, 4 * share :].reshape(seq, count, tok_count)
    cosine, sine = rope_tables(places.reshape(-1))
    order = jnp.arange(seq * tok_count, dtype=jnp.int32).reshape(seq, 1, tok_count)
    starts = jnp.moveaxis(order - places.astype(jnp.int32), 0, 1).reshape(count, 1, seq * tok_count)

    def columns(weight):
        part = weight.reshape(share, fsdp * groups, GROUP, down_share)
        part = jnp.moveaxis(part, 2, 0).reshape(1, GROUP, share, hidden_width)
        part = jnp.broadcast_to(part, (groups, GROUP, share, hidden_width))
        part = part.reshape(seq * share, hidden_width)
        return lax.all_to_all(part, "seq", split_axis=0, concat_axis=0, tiled=True)

    inputs_all = after(inputs_all, qkv_weight, cosine, sine, starts, gains)
    g_part = columns(after(w_gate, inputs_all))
    o_weight = lax.all_gather(w_output, BOTH, axis=0, tiled=True)
    proj, squares = project(inputs_all, qkv_weight)
    scales = lax.rsqrt(sum_small(squares[:2], "seq") / width + EPSILON).T
    rotated = prepare(proj, scales, qk_gain, cosine, sine)
    g_part = after(g_part, *rotated)
    u_part = columns(after(w_up, g_part))
    g_weight = lax.all_gather(g_part, "fsdp", axis=0, tiled=True)
    rotated = [v.reshape(head_shape) for v in rotated]
    attended, log_sums = attend_forward(*rotated, starts, factor)
    attended = after(attended, u_part)
    attn_rows = lax.all_to_all(
        attended.reshape(seq, own_rows, local_width), "seq", split_axis=0, concat_axis=0, tiled=True
    )
    attn_rows = jnp.moveaxis(attn_rows, 0, 1).reshape(own_rows, width)

    a_proj = dot_nn(attn_rows, o_weight)
    a_scale = inv_rms(a_proj)
    hidden = inputs.astype(F32) + a_proj * a_scale * a_gain
    d_part = gather_outer(after(w_down, u_part))
    u_weight, d_weight = (lax.all_gather(v, "fsdp", axis=0, tiled=True) for v in (u_part, d_part))
    hidden_low = gather_group(hidden.astype(BF16))
    gate, up, act = gate_up(hidden_low, g_weight, u_weight)
    m_proj = scatter_far(scatter_near(down(act, d_weight)))
    m_scale = inv_rms(m_proj)
    mixed = (hidden + m_proj * m_scale * m_gain).astype(BF16)

    grad_mproj, grad_mgain = norm_back(grad_rows, m_proj, m_scale, m_gain)
    grad_mproj = gather_group(grad_mproj.astype(BF16))

    def over_rows(part):
        return lax.psum_scatter(part, "fsdp", scatter_dimension=0, tiled=True)

    def columns_sent(part):
        return lax.all_to_all(part, "seq", split_axis=0, concat_axis=0, tiled=True)

    def columns_joined(part):
        part = part.reshape(groups, GROUP, share, fsdp * groups, down_share)
        return jnp.moveaxis(part.astype(F32).sum(axis=0), 0, 2).reshape(share, -1)

    dgate, dup = act_back(grad_mproj, d_weight, gate, up)
    down_grad = weight_grad(act, grad_mproj, dgate)
    share_down = over_rows(down_grad)
    grads = hidden_back(dgate, g_weight, dup, u_weight, down_grad)
    grads = scatter_near(grads)
    gate_grad = weight_grad(hidden_low, dgate, grads)
    share_gate = over_rows(gate_grad)
    grad_hidden = grad_rows + scatter_far(grads, gate_grad)

    grad_aproj, grad_again = norm_back(grad_hidden, a_proj, a_scale, a_gain)
    grad_aproj = after(grad_aproj.astype(BF16), share_down)
    grad_attn = dot_nt(grad_aproj, o_weight).astype(BF16)
    grad_attn = jnp.moveaxis(grad_attn.reshape(own_rows, seq, local_width), 1, 0)
    grad_heads = lax.all_to_all(grad_attn, "seq", split_axis=0, concat_axis=0, tiled=True)
    up_grad = weight_grad(hidden_low, dup, gate_grad, grad_attn)
    share_up = over_rows(up_grad)
    o_grad = weight_grad(attn_rows, grad_aproj, up_grad)
    share_output = over_rows(o_grad)
    grad_heads = after(grad_heads, o_grad)
    share_down = scatter_outer(after(share_down, grad_heads))
    dq, dk, dv = attend_backward(
        *rotated, starts, grad_heads.reshape(head_shape), log_sums, factor
    )
    dq = after(dq, share_down)
    share_gate = columns_sent(after(share_gate, dq))
    dq, dk, dv = (v.reshape(seq * own_rows, local_width) for v in (dq, dk, dv))
    q_rot, k_rot = (v.reshape(seq * own_rows, local_width) for v in rotated[:2])
    inner = jnp.stack(
        [
            jnp.sum(dq.astype(F32) * q_rot.astype(F32), axis=1),
            jnp.sum(dk.astype(F32) * k_rot.astype(F32), axis=1),
        ]
    )
    inner = sum_small(inner, "seq") / width
    grad_qkv, gain_sums = unprepare(
        dq, dk, after(dv, share_up), proj, scales, inner.T, qk_gain, cosine, sine
    )
    partial = dot_nt(grad_qkv, qkv_weight).astype(BF16)
    partial = after(partial, share_gate)
    qkv_grad = weight_grad(inputs_all, grad_qkv, partial)
    qkv_grad = after(qkv_grad, share_output)
    share_output = lax.all_to_all(share_output, "seq", split_axis=0, concat_axis=0, tiled=True)
    middle = (share_output,)
    share_output = share_output.astype(F32).reshape(seq, share, width).sum(axis=0)
    share_gate = columns_joined(share_gate)
    share_up = columns_sent(after(share_up, partial))
    early = (share_up,)
    share_up = columns_joined(share_up)
    share_qkv = over_rows(qkv_grad)
    share_qkv = lax.all_to_all(
        share_qkv.reshape(seq, share, 3 * local_width), "seq", split_axis=0, concat_axis=0, tiled=True
    )
    middle += (share_qkv,)
    share_qkv = share_qkv.reshape(seq, share, 3, local_width).transpose(2, 1, 0, 3)
    share_qkv = share_qkv.reshape(3, share, width).astype(F32)
    slots = lax.dynamic_update_slice_in_dim(
        jnp.zeros((2, width), F32), gain_sums.reshape(2, local_width), place * local_width, 1
    )
    slots = jnp.concatenate([slots, grad_again[None], grad_mgain[None]])
    slots = sum_small(sum_small(slots, "fsdp"), "seq")
    gain_grads = lax.dynamic_slice_in_dim(slots, (row * seq + place) * share, share, 1)
    late = (share_gate, share_up, share_output, share_qkv, gain_grads)
    grad_inputs = scatter_line(partial, {1: early, 2: middle, seq // 2 - 1: late})
    input_grad = (grad_hidden + grad_inputs).astype(BF16)
    return (
        mixed.reshape(tokens.shape),
        input_grad.reshape(tokens.shape),
        share_qkv[0],
        share_qkv[1],
        share_qkv[2],
        share_output,
        gain_grads[0],
        gain_grads[1],
        gain_grads[2],
        share_gate,
        share_up,
        share_down,
        gain_grads[3],
    )


def solution(mesh):
    rows = P(BOTH, None)
    flat = P(BOTH)
    acts = P(None, "fsdp", "seq", None)
    return jax.shard_map(
        on_device,
        mesh=mesh,
        in_specs=(acts, P(None, "fsdp", "seq"), acts, rows, rows, rows, rows, flat, flat, flat)
        + (rows, rows, rows, flat),
        out_specs=(acts, acts, rows, rows, rows, rows, flat, flat, flat, rows, rows, rows, flat),
        check_vma=False,
    )
```

```python
import functools

import jax
import jax.numpy as jnp
from jax import lax
from jax.experimental import pallas as pl
from jax.experimental.pallas import tpu as pltpu
from jax.sharding import PartitionSpec as P

HEADS = 16
HEAD_DIM = 128

EPSILON = 1e-06
THETA = 500000.0

BF16 = jnp.bfloat16
F32 = jnp.float32
BOTH = ("fsdp", "seq")

GROUP = 4

UNREAD = pl.BlockSpec(memory_space=pl.ANY)
NO_COST = pl.CostEstimate(flops=0, bytes_accessed=0, transcendentals=0)


def cost(flops):
    return pl.CostEstimate(flops=int(flops * 1), bytes_accessed=0, transcendentals=0)


def dot_nn(former, latter):
    return jnp.dot(former, latter, preferred_element_type=F32)


def dot_tn(former, latter):
    return lax.dot_general(former, latter, (((0,), (0,)), ((), ())), preferred_element_type=F32)


def dot_nt(former, latter):
    return lax.dot_general(former, latter, (((1,), (1,)), ((), ())), preferred_element_type=F32)


def inv_rms(values):
    return lax.rsqrt(jnp.mean(values * values, axis=-1, keepdims=True) + EPSILON)


def norm_back(incoming, values, factor, gain_row):
    weighted = incoming * gain_row
    inner_mean = jnp.mean(weighted * values, axis=-1, keepdims=True)
    result_grad = factor * (weighted - values * factor * factor * inner_mean)
    return (result_grad, jnp.sum(incoming * values * factor, axis=0))


def rope_tables(places_pos):
    half = HEAD_DIM // 2
    exponent = jnp.arange(0, half, dtype=F32) * (2.0 / HEAD_DIM)
    frequency = THETA ** (-exponent)
    angles = places_pos.astype(F32)[:, None] * frequency[None, :]
    cosine, sine = jnp.cos(angles), jnp.sin(angles)
    return (
        jnp.concatenate([cosine, cosine], axis=-1),
        jnp.concatenate([-sine, sine], axis=-1),
    )


def bits_of(size):
    return [1 << i for i in range(size.bit_length() - 1)]


def exchange(values, axis, bit):
    return lax.ppermute(values, axis, [(i, i ^ bit) for i in range(lax.axis_size(axis))])


def sum_small(values, axis):
    for bit in bits_of(lax.axis_size(axis)):
        values = values + exchange(values, axis, bit)
    return values


def after(values, *earlier):
    return pl.pallas_call(
        lambda *refs: None,
        in_specs=[UNREAD] * (1 + len(earlier)),
        out_specs=UNREAD,
        out_shape=jax.ShapeDtypeStruct(values.shape, values.dtype),
        input_output_aliases={0: 0},
        cost_estimate=NO_COST,
    )(values, *earlier)


def gather_group(values):
    near, far = 1, 2
    other = exchange(values, "seq", far)
    return jnp.concatenate(
        [values, other, exchange(values, "seq", near), exchange(other, "seq", near)]
    )


def halve(held, bits, axis, stride=1):
    for i, bit in enumerate(bits):
        sent = {m: exchange(v, axis, bit * stride) for m, v in held.items() if m & bit}
        held = {m: held[m].astype(F32) + sent[m ^ bit].astype(F32) for m in held if not m & bit}
        if i < len(bits) - 1:
            held = {m: v.astype(BF16) for m, v in held.items()}
    return held[0]


def scatter_near(values):
    rows = values.shape[0] // 2
    return values[:rows].astype(F32) + exchange(values[rows:], "seq", 1).astype(F32)


def scatter_far(half, *earlier):
    rows = half.shape[0] // 2
    return half[:rows] + after(exchange(half[rows:].astype(BF16), "seq", 2), *earlier).astype(F32)


def gather_outer(values):
    groups = lax.axis_size("seq") // GROUP
    own = lax.axis_index("seq") // GROUP
    found = {0: values}
    for bit in bits_of(groups):
        found |= {m ^ bit: exchange(v, "seq", bit * GROUP) for m, v in found.items()}
    blocks = []
    for i in range(groups):
        block = found[0]
        for m in range(1, groups):
            block = jnp.where((own ^ i) == m, found[m], block)
        blocks.append(block)
    return jnp.concatenate(blocks)


def scatter_outer(values):
    groups = lax.axis_size("seq") // GROUP
    own = lax.axis_index("seq") // GROUP
    rows = values.shape[0] // groups
    held = {
        m: lax.dynamic_slice_in_dim(values, (own ^ m) * rows, rows, 0) for m in range(groups)
    }
    return halve(held, bits_of(groups)[::-1], "seq", GROUP)


def shift(values, step):
    size = lax.axis_size("seq")
    pairs = [(i, i + 2 * step) for i in range(size) if 0 <= i + 2 * step < size]
    return lax.ppermute(values, "seq", pairs)


def gather_placed(values, axis):
    size, own = lax.axis_size(axis), lax.axis_index(axis)
    bits, rows = bits_of(size), values.shape[0]
    parts = [(0, values, bits[::-1])]
    if axis == "fsdp":
        half = rows // 2
        parts = [(0, values[:half], bits), (half, values[half:], bits[::-1])]
    out = jnp.zeros((size * rows, values.shape[1]), values.dtype)
    for first, part, order in parts:
        found = {0: part}
        for bit in order:
            found |= {m ^ bit: exchange(v, axis, bit) for m, v in found.items()}
        for m, v in found.items():
            out = lax.dynamic_update_slice_in_dim(out, v, (own ^ m) * rows + first, 0)
    return out


def scatter_line(values, earlier):
    size, place = lax.axis_size("seq"), lax.axis_index("seq")
    pairs, pair, core = size // 2, place // 2, place % 2
    rows = values.shape[0] // size
    blocks = values.reshape(pairs, 2, rows, values.shape[1])
    sent = exchange(lax.dynamic_index_in_dim(blocks, 1 - core, 1, keepdims=False), "seq", 1)
    kept = lax.dynamic_index_in_dim(blocks, core, 1, keepdims=False)
    blocks = (kept.astype(F32) + sent.astype(F32)).astype(BF16)

    def block_at(place):
        place = jnp.clip(place, 0, pairs - 1)
        return lax.dynamic_index_in_dim(blocks, place, 0, keepdims=False)

    up = down = None
    for far in range(pairs - 1, 0, -1):
        next_up, next_down = block_at(pair + far), block_at(pair - far)
        if up is not None:
            next_up = (next_up.astype(F32) + up.astype(F32)).astype(BF16)
            next_down = (next_down.astype(F32) + down.astype(F32)).astype(BF16)
        up, down = shift(next_up, 1), shift(next_down, -1)
        up = after(up, down, *earlier.get(pairs - far, ()))
    return block_at(pair).astype(F32) + up.astype(F32) + down.astype(F32)


def ordered(kernel, count, earlier):
    return lambda *refs: kernel(*refs[:count], *refs[count + len(earlier) :])


def gate_up_kernel(rows_ref, gate_ref, up_ref, gate_out, up_out, act_out):
    gate = dot_nn(rows_ref[...], gate_ref[...])
    up = dot_nn(rows_ref[...], up_ref[...])
    gate_out[...] = gate.astype(BF16)
    up_out[...] = up.astype(BF16)
    act_out[...] = (gate * jax.nn.sigmoid(gate) * up).astype(BF16)


def down_kernel(act_ref, down_ref, out_ref):
    out_ref[...] = dot_nn(act_ref[...], down_ref[...]).astype(BF16)


def act_back_kernel(grad_ref, down_ref, gate_ref, up_ref, dgate_ref, dup_ref):
    dact = dot_nt(grad_ref[...], down_ref[...])
    gate, up = gate_ref[...].astype(F32), up_ref[...].astype(F32)
    sigmoid = jax.nn.sigmoid(gate)
    dgate_ref[...] = (dact * up * sigmoid * (1.0 + gate * (1.0 - sigmoid))).astype(BF16)
    dup_ref[...] = (dact * gate * sigmoid).astype(BF16)


def hidden_back_kernel(dgate_ref, gate_ref, dup_ref, up_ref, out_ref):
    total = dot_nt(dgate_ref[...], gate_ref[...]) + dot_nt(dup_ref[...], up_ref[...])
    out_ref[...] = total.astype(BF16)


def weight_kernel(former_ref, latter_ref, out_ref):
    out_ref[...] = dot_tn(former_ref[...], latter_ref[...]).astype(BF16)


def held_rows(values):
    return pl.BlockSpec((min(1024, values.shape[0]), values.shape[1]), lambda j, i: (i, 0))


def cols_of(values, block):
    return pl.BlockSpec((values.shape[0], block), lambda j, i: (0, j))


def rows_of(values, block):
    return pl.BlockSpec((block, values.shape[1]), lambda j, i: (j, 0))


def tiles_of(values, block):
    return pl.BlockSpec((min(1024, values.shape[0]), block), lambda j, i: (i, j))


def by_columns(kernel, operands, specs, outs, cols, earlier, products=1):
    rows = operands[0].shape[0]
    high = min(1024, rows)
    return pl.pallas_call(
        ordered(kernel, len(operands), earlier),
        grid=(cols // 512, rows // high),
        in_specs=specs + [UNREAD] * len(earlier),
        out_specs=[pl.BlockSpec((high, 512), lambda j, i: (i, j))] * outs,
        out_shape=[jax.ShapeDtypeStruct((rows, cols), BF16)] * outs,
        compiler_params=pltpu.CompilerParams(vmem_limit_bytes=56 << 20),
        cost_estimate=cost(products * rows * cols * operands[0].shape[1] * 2),
    )(*operands, *earlier)


def gate_up(rows, gate, up, *earlier):
    specs = [held_rows(rows), cols_of(gate, 512), cols_of(up, 512)]
    return by_columns(gate_up_kernel, (rows, gate, up), specs, 3, gate.shape[1], earlier, 2)


def down(act, weight, *earlier):
    specs = [held_rows(act), cols_of(weight, 512)]
    return by_columns(down_kernel, (act, weight), specs, 1, weight.shape[1], earlier)[0]


def act_back(grads, weight, gate, up, *earlier):
    specs = [held_rows(grads), rows_of(weight, 512), tiles_of(gate, 512), tiles_of(up, 512)]
    return by_columns(act_back_kernel, (grads, weight, gate, up), specs, 2, gate.shape[1], earlier)


def hidden_back(dgate, gate, dup, up, *earlier):
    specs = [held_rows(dgate), rows_of(gate, 512), held_rows(dup), rows_of(up, 512)]
    return by_columns(hidden_back_kernel, (dgate, gate, dup, up), specs, 1, gate.shape[0], earlier, 2)[0]


def weight_grad(former, latter, *earlier):
    rows, cols = former.shape[1], latter.shape[1]
    block = min(512, rows)
    specs = [
        pl.BlockSpec((former.shape[0], block), lambda j: (0, j)),
        pl.BlockSpec(latter.shape, lambda j: (0, 0)),
    ]
    return pl.pallas_call(
        ordered(weight_kernel, 2, earlier),
        grid=(rows // block,),
        in_specs=specs + [UNREAD] * len(earlier),
        out_specs=pl.BlockSpec((block, cols), lambda j: (j, 0)),
        out_shape=jax.ShapeDtypeStruct((rows, cols), BF16),
        compiler_params=pltpu.CompilerParams(vmem_limit_bytes=56 << 20),
        cost_estimate=cost(former.shape[0] * rows * cols * 2),
    )(former, latter, *earlier)


def project_kernel(rows_ref, weight_ref, out_ref, squares_ref):
    width = weight_ref.shape[1] // 3
    proj = dot_nn(rows_ref[...], weight_ref[...])
    out_ref[...] = proj
    squares = (proj[:, : 2 * width] * proj[:, : 2 * width]).astype(BF16)
    part = lax.broadcasted_iota(jnp.int32, (8, 2 * width), 1) // width
    chosen = part == lax.broadcasted_iota(jnp.int32, (8, 2 * width), 0)
    squares_ref[...] = dot_nt(chosen.astype(BF16), squares)


def project(rows, weight):
    count, depth = rows.shape
    block = min(512, count)
    cols = weight.shape[1]
    return pl.pallas_call(
        project_kernel,
        grid=(count // block,),
        in_specs=[
            pl.BlockSpec((block, depth), lambda i: (i, 0)),
            pl.BlockSpec(weight.shape, lambda i: (0, 0)),
        ],
        out_specs=[
            pl.BlockSpec((block, cols), lambda i: (i, 0)),
            pl.BlockSpec((8, block), lambda i: (0, i)),
        ],
        out_shape=[
            jax.ShapeDtypeStruct((count, cols), F32),
            jax.ShapeDtypeStruct((8, count), F32),
        ],
        compiler_params=pltpu.CompilerParams(vmem_limit_bytes=48 << 20),
        cost_estimate=cost(count * depth * cols * 2),
    )(rows, weight)


def prepare_kernel(proj_ref, scale_ref, gain_ref, cos_ref, sin_ref, q_ref, k_ref, v_ref):
    width = q_ref.shape[1]
    cosine, sine = cos_ref[...], sin_ref[...]
    for part, out_ref in ((0, q_ref), (1, k_ref)):
        scale = scale_ref[:, part : part + 1]
        for low in range(0, width, HEAD_DIM):
            cols = slice(part * width + low, part * width + low + HEAD_DIM)
            normed = proj_ref[:, cols] * scale * gain_ref[:, cols]
            turned = normed * cosine + pltpu.roll(normed, HEAD_DIM // 2, 1) * sine
            out_ref[:, low : low + HEAD_DIM] = turned.astype(BF16)
    v_ref[...] = proj_ref[:, 2 * width :].astype(BF16)


def prepare(proj, scales, gains, cosine, sine):
    rows, width3 = proj.shape
    width = width3 // 3
    block = min(512, rows)
    by_rows = lambda cols: pl.BlockSpec((block, cols), lambda i: (i, 0))
    return pl.pallas_call(
        prepare_kernel,
        grid=(rows // block,),
        in_specs=[
            by_rows(width3),
            by_rows(2),
            pl.BlockSpec((1, 2 * width), lambda i: (0, 0)),
            by_rows(HEAD_DIM),
            by_rows(HEAD_DIM),
        ],
        out_specs=[by_rows(width)] * 3,
        out_shape=[jax.ShapeDtypeStruct((rows, width), BF16)] * 3,
        cost_estimate=cost(rows * width3 * 3600),
    )(proj, scales, gains, cosine, sine)


def unprepare_kernel(
    dq_ref, dk_ref, dv_ref, proj_ref, scale_ref, inner_ref, gain_ref, cos_ref, sin_ref, out_ref, sum_ref
):
    width = dq_ref.shape[1]

    @pl.when(pl.program_id(0) == 0)
    def _():
        sum_ref[...] = jnp.zeros_like(sum_ref)

    cosine, sine = cos_ref[...], sin_ref[...]
    for part, in_ref in ((0, dq_ref), (1, dk_ref)):
        scale = scale_ref[:, part : part + 1]
        inner = inner_ref[:, part : part + 1]
        for low in range(0, width, HEAD_DIM):
            cols = slice(part * width + low, part * width + low + HEAD_DIM)
            turned = in_ref[:, low : low + HEAD_DIM].astype(F32)
            normed = turned * cosine - pltpu.roll(turned, HEAD_DIM // 2, 1) * sine
            scaled = proj_ref[:, cols] * scale
            sum_ref[:, cols] += jnp.sum(normed * scaled, axis=0, keepdims=True)
            result = scale * (normed * gain_ref[:, cols] - scaled * inner)
            out_ref[:, cols] = result.astype(BF16)
    out_ref[:, 2 * width :] = dv_ref[...]


def unprepare(dq, dk, dv, proj, scales, inner, gains, cosine, sine):
    rows, width3 = proj.shape
    width = width3 // 3
    block = min(512, rows)
    by_rows = lambda cols: pl.BlockSpec((block, cols), lambda i: (i, 0))
    fixed = pl.BlockSpec((1, 2 * width), lambda i: (0, 0))
    return pl.pallas_call(
        unprepare_kernel,
        grid=(rows // block,),
        in_specs=[by_rows(width)] * 3
        + [by_rows(width3), by_rows(2), by_rows(2), fixed, by_rows(HEAD_DIM), by_rows(HEAD_DIM)],
        out_specs=[by_rows(width3), fixed],
        out_shape=[
            jax.ShapeDtypeStruct((rows, width3), BF16),
            jax.ShapeDtypeStruct((1, 2 * width), F32),
        ],
        cost_estimate=cost(rows * width3 * 4700),
    )(dq, dk, dv, proj, scales, inner, gains, cosine, sine)


def visible_mask(first, keys, rows, starts):
    key_ids = lax.broadcasted_iota(jnp.int32, (keys, rows), 0)
    query_ids = first + lax.broadcasted_iota(jnp.int32, (keys, rows), 1)
    return (key_ids <= query_ids) & (key_ids >= starts)


def forward_kernel(q_ref, k_ref, v_ref, start_ref, o_ref, lse_ref, *, factor, blocks):
    block = lse_ref.shape[-1]
    whole = blocks * block
    for turn in range(blocks):

        @pl.when(pl.program_id(2) == turn)
        def _():
            keys = (turn + 1) * block
            queries = q_ref[...].reshape(block, HEAD_DIM)
            keys_all = k_ref[...].reshape(whole, HEAD_DIM)[:keys]
            values = v_ref[...].reshape(whole, HEAD_DIM)[:keys]
            scores = dot_nt(keys_all, queries) * factor
            visible = visible_mask(turn * block, keys, block, start_ref[0])
            scores = jnp.where(visible, scores, -1e30)
            top = jnp.max(scores, axis=0, keepdims=True)
            expo = jnp.exp(scores - top)
            total = jnp.sum(expo, axis=0, keepdims=True)
            outcome = dot_tn(values, expo.astype(BF16)) / total
            o_ref[...] = outcome.T.astype(BF16).reshape(o_ref.shape)
            lse_ref[0, 0] = top + jnp.log(total)


def backward_kernel(
    q_ref, k_ref, v_ref, start_ref, do_ref, lse_ref, dq_ref, dk_ref, dv_ref, dk_sum, dv_sum, *, factor, blocks
):
    block = lse_ref.shape[-1]
    whole = blocks * block

    @pl.when(pl.program_id(2) == 0)
    def _():
        dk_sum[...] = jnp.zeros_like(dk_sum)
        dv_sum[...] = jnp.zeros_like(dv_sum)

    for turn in range(blocks):

        @pl.when(pl.program_id(2) == turn)
        def _():
            keys = (turn + 1) * block
            queries = q_ref[...].reshape(block, HEAD_DIM)
            grads = do_ref[...].reshape(block, HEAD_DIM)
            keys_all = k_ref[...].reshape(whole, HEAD_DIM)[:keys]
            values = v_ref[...].reshape(whole, HEAD_DIM)[:keys]
            scores = dot_nt(keys_all, queries) * factor
            visible = visible_mask(turn * block, keys, block, start_ref[0])
            soft = jnp.where(visible, jnp.exp(scores - lse_ref[0, 0]), 0.0)
            dv_sum[:keys] += dot_nn(soft.astype(BF16), grads)
            dsoft = dot_nt(values, grads)
            delta = jnp.sum(dsoft * soft, axis=0, keepdims=True)
            dscores = (soft * (dsoft - delta)).astype(BF16)
            dk_sum[:keys] += dot_nn(dscores, queries)
            dq = dot_tn(keys_all, dscores) * factor
            dq_ref[...] = dq.T.astype(BF16).reshape(dq_ref.shape)

    @pl.when(pl.program_id(2) == blocks - 1)
    def _():
        dk_ref[...] = (dk_sum[...] * factor).astype(BF16).reshape(dk_ref.shape)
        dv_ref[...] = dv_sum[...].astype(BF16).reshape(dv_ref.shape)


def attention_specs(shape):
    groups, count, rows, width = shape
    whole = groups * rows
    block = min(512, whole)
    per = block // rows
    some = pl.BlockSpec((per, 1, rows, HEAD_DIM), lambda b, h, i: (i, b, 0, h))
    every = pl.BlockSpec((groups, 1, rows, HEAD_DIM), lambda b, h, i: (0, b, 0, h))
    starts = pl.BlockSpec((1, 1, block), lambda b, h, i: (b, 0, i))
    sums = pl.BlockSpec((1, 1, 1, block), lambda b, h, i: (b, h, 0, i))
    heads = width // HEAD_DIM
    pairs = count * heads * whole * whole
    return some, every, starts, sums, (count, heads, whole // block), whole, pairs


def attend_forward(queries, keys, values, starts, factor, *earlier):
    some, every, start_spec, sums, grid, whole, pairs = attention_specs(queries.shape)
    return pl.pallas_call(
        ordered(functools.partial(forward_kernel, factor=factor, blocks=grid[2]), 4, earlier),
        grid=grid,
        in_specs=[some, every, every, start_spec] + [UNREAD] * len(earlier),
        out_specs=[some, sums],
        out_shape=[
            jax.ShapeDtypeStruct(queries.shape, BF16),
            jax.ShapeDtypeStruct((grid[0], grid[1], 1, whole), F32),
        ],
        compiler_params=pltpu.CompilerParams(vmem_limit_bytes=48 << 20),
        cost_estimate=cost(pairs * HEAD_DIM * 11),
    )(queries, keys, values, starts, *earlier)


def attend_backward(queries, keys, values, starts, grads, log_sums, factor, *earlier):
    some, every, start_spec, sums, grid, whole, pairs = attention_specs(queries.shape)
    return pl.pallas_call(
        ordered(functools.partial(backward_kernel, factor=factor, blocks=grid[2]), 6, earlier),
        grid=grid,
        in_specs=[some, every, every, start_spec, some, sums] + [UNREAD] * len(earlier),
        out_specs=[some, every, every],
        out_shape=[jax.ShapeDtypeStruct(queries.shape, BF16)] * 3,
        scratch_shapes=[pltpu.VMEM((whole, HEAD_DIM), F32)] * 2,
        compiler_params=pltpu.CompilerParams(vmem_limit_bytes=52 << 20),
        cost_estimate=cost(pairs * HEAD_DIM * 20),
    )(queries, keys, values, starts, grads, log_sums, *earlier)


def on_device(
    tokens,
    positions,
    out_grad,
    w_query,
    w_key,
    w_value,
    w_output,
    query_gain,
    key_gain,
    attn_gain,
    w_gate,
    w_up,
    w_down,
    mlp_gain,
):
    fsdp, seq = lax.axis_size("fsdp"), lax.axis_size("seq")
    row, place = lax.axis_index("fsdp"), lax.axis_index("seq")
    groups = seq // GROUP
    factor = HEAD_DIM ** (-0.5)
    count = tokens.shape[0] * tokens.shape[1]
    tok_count, width = tokens.shape[2], tokens.shape[3]
    own_rows = count * tok_count
    local_width = width // seq
    hidden_width = w_gate.shape[1] // GROUP
    share = w_query.shape[0]
    down_share = w_down.shape[0]
    head_shape = (seq, count, tok_count, local_width)

    inputs = tokens.reshape(own_rows, width)
    grad_rows = out_grad.reshape(own_rows, width).astype(F32)
    inputs_all = lax.all_gather(inputs, "seq", axis=0, tiled=True)

    qkv_weight = lax.all_to_all(
        jnp.stack([w_query, w_key, w_value]), "seq", split_axis=2, concat_axis=1, tiled=True
    )
    qkv_weight = jnp.moveaxis(qkv_weight, 0, 1).reshape(seq * share, 3 * local_width)
    qkv_weight = gather_placed(qkv_weight, "fsdp")

    own_gains = jnp.stack([query_gain, key_gain, attn_gain, mlp_gain]).astype(F32)
    small = jnp.concatenate([own_gains.reshape(-1), positions.reshape(-1).astype(F32)])
    small = lax.dynamic_update_index_in_dim(jnp.zeros((seq, small.shape[0]), F32), small, place, 0)
    small = sum_small(small, "seq")
    gains = small[:, : 4 * share].reshape(seq, 4, share)
    gains = lax.dynamic_update_index_in_dim(jnp.zeros((fsdp, seq, 4, share), F32), gains, row, 0)
    gains = jnp.moveaxis(sum_small(gains, "fsdp"), 2, 0).reshape(4, 1, width)
    a_gain, m_gain = gains[2], gains[3]
    qk_gain = lax.dynamic_slice_in_dim(gains[:2], place * local_width, local_width, 2)
    qk_gain = qk_gain.reshape(1, 2 * local_width)
    places = small[:, 4 * share :].reshape(seq, count, tok_count)
    cosine, sine = rope_tables(places.reshape(-1))
    order = jnp.arange(seq * tok_count, dtype=jnp.int32).reshape(seq, 1, tok_count)
    starts = jnp.moveaxis(order - places.astype(jnp.int32), 0, 1).reshape(count, 1, seq * tok_count)

    def columns(weight):
        part = weight.reshape(share, fsdp * groups, GROUP, down_share)
        part = jnp.moveaxis(part, 2, 0).reshape(1, GROUP, share, hidden_width)
        part = jnp.broadcast_to(part, (groups, GROUP, share, hidden_width))
        part = part.reshape(seq * share, hidden_width)
        return lax.all_to_all(part, "seq", split_axis=0, concat_axis=0, tiled=True)

    inputs_all = after(inputs_all, qkv_weight, cosine, sine, starts, gains)
    g_part = columns(after(w_gate, inputs_all))
    o_weight = lax.all_gather(w_output, BOTH, axis=0, tiled=True)
    proj, squares = project(inputs_all, qkv_weight)
    scales = lax.rsqrt(sum_small(squares[:2], "seq") / width + EPSILON).T
    rotated = prepare(proj, scales, qk_gain, cosine, sine)
    g_part = after(g_part, *rotated)
    u_part = columns(after(w_up, g_part))
    g_weight = lax.all_gather(g_part, "fsdp", axis=0, tiled=True)
    rotated = [v.reshape(head_shape) for v in rotated]
    attended, log_sums = attend_forward(*rotated, starts, factor)
    attended = after(attended, u_part)
    attn_rows = lax.all_to_all(
        attended.reshape(seq, own_rows, local_width), "seq", split_axis=0, concat_axis=0, tiled=True
    )
    attn_rows = jnp.moveaxis(attn_rows, 0, 1).reshape(own_rows, width)

    a_proj = dot_nn(attn_rows, o_weight)
    a_scale = inv_rms(a_proj)
    hidden = inputs.astype(F32) + a_proj * a_scale * a_gain
    d_part = gather_outer(after(w_down, u_part))
    u_weight, d_weight = (lax.all_gather(v, "fsdp", axis=0, tiled=True) for v in (u_part, d_part))
    hidden_low = gather_group(hidden.astype(BF16))
    gate, up, act = gate_up(hidden_low, g_weight, u_weight)
    m_proj = scatter_far(scatter_near(down(act, d_weight)))
    m_scale = inv_rms(m_proj)
    mixed = (hidden + m_proj * m_scale * m_gain).astype(BF16)

    grad_mproj, grad_mgain = norm_back(grad_rows, m_proj, m_scale, m_gain)
    grad_mproj = gather_group(grad_mproj.astype(BF16))

    def over_rows(part):
        return lax.psum_scatter(part, "fsdp", scatter_dimension=0, tiled=True)

    def columns_sent(part):
        return lax.all_to_all(part, "seq", split_axis=0, concat_axis=0, tiled=True)

    def columns_joined(part):
        part = part.reshape(groups, GROUP, share, fsdp * groups, down_share)
        return jnp.moveaxis(part.astype(F32).sum(axis=0), 0, 2).reshape(share, -1)

    dgate, dup = act_back(grad_mproj, d_weight, gate, up)
    down_grad = weight_grad(act, grad_mproj, dgate)
    share_down = over_rows(down_grad)
    grads = hidden_back(dgate, g_weight, dup, u_weight, down_grad)
    gate_grad = weight_grad(hidden_low, dgate, grads)
    grads = scatter_near(grads)
    up_grad = weight_grad(hidden_low, dup, gate_grad, grads)
    share_gate = over_rows(gate_grad)
    grad_hidden = grad_rows + scatter_far(grads, up_grad)

    grad_aproj, grad_again = norm_back(grad_hidden, a_proj, a_scale, a_gain)
    grad_aproj = after(grad_aproj.astype(BF16), share_down)
    grad_attn = dot_nt(grad_aproj, o_weight).astype(BF16)
    grad_attn = jnp.moveaxis(grad_attn.reshape(own_rows, seq, local_width), 1, 0)
    grad_heads = lax.all_to_all(grad_attn, "seq", split_axis=0, concat_axis=0, tiled=True)
    share_up = over_rows(up_grad)
    o_grad = weight_grad(attn_rows, grad_aproj, grad_attn)
    share_output = over_rows(o_grad)
    grad_heads = after(grad_heads, o_grad)
    share_down = scatter_outer(after(share_down, grad_heads))
    dq, dk, dv = attend_backward(
        *rotated, starts, grad_heads.reshape(head_shape), log_sums, factor
    )
    dq = after(dq, share_down)
    share_gate = columns_sent(after(share_gate, dq))
    dq, dk, dv = (v.reshape(seq * own_rows, local_width) for v in (dq, dk, dv))
    q_rot, k_rot = (v.reshape(seq * own_rows, local_width) for v in rotated[:2])
    inner = jnp.stack(
        [
            jnp.sum(dq.astype(F32) * q_rot.astype(F32), axis=1),
            jnp.sum(dk.astype(F32) * k_rot.astype(F32), axis=1),
        ]
    )
    inner = sum_small(inner, "seq") / width
    grad_qkv, gain_sums = unprepare(
        dq, dk, after(dv, share_up), proj, scales, inner.T, qk_gain, cosine, sine
    )
    partial = dot_nt(grad_qkv, qkv_weight).astype(BF16)
    partial = after(partial, share_gate)
    qkv_grad = weight_grad(inputs_all, grad_qkv, partial)
    qkv_grad = after(qkv_grad, share_output)
    share_output = lax.all_to_all(share_output, "seq", split_axis=0, concat_axis=0, tiled=True)
    middle = (share_output,)
    share_output = share_output.astype(F32).reshape(seq, share, width).sum(axis=0)
    share_gate = columns_joined(share_gate)
    share_up = columns_sent(after(share_up, partial))
    early = (share_up,)
    share_up = columns_joined(share_up)
    share_qkv = over_rows(qkv_grad)
    share_qkv = lax.all_to_all(
        share_qkv.reshape(seq, share, 3 * local_width), "seq", split_axis=0, concat_axis=0, tiled=True
    )
    share_qkv = share_qkv.reshape(seq, share, 3, local_width).transpose(2, 1, 0, 3)
    share_qkv = share_qkv.reshape(3, share, width).astype(F32)
    slots = lax.dynamic_update_slice_in_dim(
        jnp.zeros((2, width), F32), gain_sums.reshape(2, local_width), place * local_width, 1
    )
    slots = jnp.concatenate([slots, grad_again[None], grad_mgain[None]])
    slots = sum_small(sum_small(slots, "fsdp"), "seq")
    gain_grads = lax.dynamic_slice_in_dim(slots, (row * seq + place) * share, share, 1)
    late = (share_gate, share_up, share_output, share_qkv, gain_grads)
    grad_inputs = scatter_line(partial, {1: early, 2: middle, seq // 2 - 1: late})
    input_grad = (grad_hidden + grad_inputs).astype(BF16)
    return (
        mixed.reshape(tokens.shape),
        input_grad.reshape(tokens.shape),
        share_qkv[0],
        share_qkv[1],
        share_qkv[2],
        share_output,
        gain_grads[0],
        gain_grads[1],
        gain_grads[2],
        share_gate,
        share_up,
        share_down,
        gain_grads[3],
    )


def solution(mesh):
    rows = P(BOTH, None)
    flat = P(BOTH)
    acts = P(None, "fsdp", "seq", None)
    return jax.shard_map(
        on_device,
        mesh=mesh,
        in_specs=(acts, P(None, "fsdp", "seq"), acts, rows, rows, rows, rows, flat, flat, flat)
        + (rows, rows, rows, flat),
        out_specs=(acts, acts, rows, rows, rows, rows, flat, flat, flat, rows, rows, rows, flat),
        check_vma=False,
    )
```
